256 devices in a mesh: gx: 128 (over x, y, z), gy: 2 (over core).
Axes of the slice: x: 4, y: 4, z: 8, core: 2. Of those that a mesh axis runs over, the one named last changes fastest.
Arguments:
- positions: float32 [3, 2, 1114112], P(None, 'gy', 'gx'), may hold values from -7 to 7
- forces: float32 [3, 2, 1114112], P(None, 'gy', 'gx'), may hold values from -6 to 6
- deriv_mat: float32 [544, 544], replicated, may hold values from -0.25 to 0.25
- quad_mat: float32 [544, 544], replicated, may hold values from -0.25 to 0.25
- point_dest: int32 [2, 1114112], P('gy', 'gx'), may hold values from 0 to 32767, as said below
- leaf_center: float32 [3, 2, 32768], P(None, 'gy', 'gx'), may hold values from -4 to 4
- tile_src: int32 [2, 4194304], P('gy', 'gx'), may hold values from 0 to 32768, as said below
- neighbours: int32 [2, 3, 32768], P('gy', None, 'gx'), may hold values from 0 to 32767, as said below
- inter_leaf: int32 [2, 8, 32768], P('gy', None, 'gx'), may hold values from 0 to 32767, as said below
- inter_op: int32 [2, 8, 32768], P('gy', None, 'gx'), may hold values from 0 to 15
- coarse_op: int32 [2, 128, 256], P('gy', 'gx'), may hold values from 0 to 16, as said below
- up_pinv: float32 [168, 168], replicated, may hold values from -0.5 to 0.5
- trans_ops: float32 [16, 168, 168], replicated, may hold values from -0.25 to 0.25
- child_ops: float32 [8, 168, 168], replicated, may hold values from -0.03125 to 0.03125
Outputs:
- velocity: float32 [3, 2, 1114112], P(None, 'gy', 'gx')
The draws below stay inside these ranges and needn't reach their ends.
Inputs may be any that keep to these rules, and one draw needn't show every extreme that they name: `point_dest`: within one slab and one column block d, the values are distinct; the slots sent to each owner are used from k = 0 without gaps; every column block fills all 256 slots of the same 128 // 8 owners. `tile_src`: each point of the slab fills exactly one leaf slot of the owner it is sent to; 32768 marks an empty slot; the busiest owners have all slots filled. `neighbours`: entry 0 is the leaf itself; the others lie within 256 leaves of it. `inter_leaf`: every entry lies within 256 leaves of its leaf. `coarse_op`: 16 marks no interaction; it stands exactly for the target box itself and the boxes of the owners next to it in the same slab.
All inputs are finite; a program needn't handle non-finite values.
Results may differ from the reference program's by a relative error of at most 0.0003.
Values sent between devices are 32-bit elements; how exact they have to be, the bound alone decides.
No kernel may reach another device: no remote copies, remote signals or barrier semaphores. Data moves between devices by JAX's collectives and lax.ppermute only.
A program may use at most 192 MiB of HBM per device.

```python
import math
import jax
import jax.numpy as jnp
from jax import lax

P_SIZE = 544
EXP = 168
SURF = 56
NOPS = 16
TILE = 128
K_NB = 3
K_IL = 8
L_DEV = 256
CAP = 256
NPD = 8704
NPS = 1114112
NLS = 32768
N_GX = 128
N_GY = 2


def slab_routing(key):
    nbusy = N_GX // 8
    nrest = N_GX - nbusy
    rest_points = NPD - nbusy * CAP
    base = rest_points // nrest
    extra = rest_points % nrest
    key_busy, key_send, key_take = jax.random.split(key, 3)
    owner_rank = jax.random.permutation(key_busy, N_GX)
    busy = owner_rank < nbusy
    rest_position = jnp.clip(jnp.cumsum((~busy).astype(jnp.int32)) - 1, 0, nrest - 1)

    def counts_for(single):
        order = jax.random.permutation(single, nrest)
        return jnp.where(busy, CAP, base + (order[rest_position] < extra).astype(jnp.int32)).astype(jnp.int32)
    send_keys = jax.random.split(key_send, N_GX)
    counts = jax.vmap(counts_for)(send_keys)

    def dest_for(single, count_row):
        inclusive = jnp.cumsum(count_row)
        exclusive = inclusive - count_row
        ranks = jnp.arange(NPD, dtype=jnp.int32)
        owner = jnp.searchsorted(inclusive, ranks, side='right').astype(jnp.int32)
        within = ranks - exclusive[owner]
        shuffle = jax.random.permutation(jax.random.fold_in(single, 7), NPD)
        return jnp.zeros((NPD,), jnp.int32).at[shuffle].set(owner * CAP + within)
    dest = jax.vmap(dest_for)(send_keys, counts)

    def tiles_for(single, count_col):
        flat = jnp.arange(N_GX * CAP, dtype=jnp.int32)
        valid = flat % CAP < count_col[flat // CAP]
        rank = jnp.clip(jnp.cumsum(valid.astype(jnp.int32)) - 1, 0, L_DEV * TILE - 1)
        slot_order = jax.random.permutation(single, L_DEV * TILE)
        target = jnp.where(valid, slot_order[rank], L_DEV * TILE).astype(jnp.int32)
        source = jnp.full((L_DEV * TILE,), N_GX * CAP, jnp.int32).at[target].set(flat, mode='drop')
        return (source, jnp.where(valid, target, 0).astype(jnp.int32))
    take_keys = jax.random.split(key_take, N_GX)
    source, slot_of = jax.vmap(tiles_for)(take_keys, counts.T)
    owner = dest // CAP
    within = dest % CAP
    sender = jnp.arange(N_GX, dtype=jnp.int32)[:, None]
    slot = slot_of[owner, sender * CAP + within]
    leaf = owner * L_DEV + slot // TILE
    return (dest.reshape(-1), source.reshape(-1), leaf.reshape(-1))


def all_routing(key):
    keys = jax.random.split(jax.random.fold_in(key, 101), N_GY)
    return jax.vmap(slab_routing)(keys)


def center_table(key):
    center_key = jax.random.fold_in(key, 202)
    return jax.random.uniform(center_key, (3, N_GY, NLS), jnp.float32, -4.0, 4.0)


def draw_point_dest(key, part):
    return all_routing(key)[0]


def draw_tile_src(key, part):
    return all_routing(key)[1]


def draw_leaf_center(key, part):
    return center_table(key)


def draw_positions(key, part):
    centers = center_table(key)
    leaf = all_routing(key)[2]
    offset_key = jax.random.fold_in(key, 303)
    offset = jax.random.uniform(offset_key, (3, N_GY, NPS), jnp.float32, -3.0, 3.0)
    placed = jnp.take_along_axis(centers, jnp.broadcast_to(leaf[None], (3, N_GY, NPS)), axis=2)
    return placed + offset


def draw_neighbours(key, part):
    moves = jax.random.randint(jax.random.fold_in(key, 404), (N_GY, K_NB - 1, NLS), -L_DEV, L_DEV + 1)
    leaf = jnp.arange(NLS, dtype=jnp.int32)
    others = jnp.clip(leaf + moves, 0, NLS - 1).astype(jnp.int32)
    return jnp.concatenate([jnp.broadcast_to(leaf, (N_GY, 1, NLS)), others], axis=1)


def draw_inter_leaf(key, part):
    moves = jax.random.randint(jax.random.fold_in(key, 454), (N_GY, K_IL, NLS), -L_DEV, L_DEV + 1)
    leaf = jnp.arange(NLS, dtype=jnp.int32)
    return jnp.clip(leaf + moves, 0, NLS - 1).astype(jnp.int32)


def draw_coarse_op(key, part):
    chosen = jax.random.randint(jax.random.fold_in(key, 505), (N_GY, N_GX, N_GX * N_GY), 0, NOPS)
    boxes = jnp.arange(N_GX * N_GY, dtype=jnp.int32)
    box_owner = boxes // N_GY
    box_slab = boxes % N_GY
    target_slab = jnp.arange(N_GY, dtype=jnp.int32)[:, None, None]
    target_owner = jnp.arange(N_GX, dtype=jnp.int32)[None, :, None]
    close = (box_slab[None, None, :] == target_slab) & (jnp.abs(box_owner[None, None, :] - target_owner) <= 1)
    return jnp.where(close, NOPS, chosen).astype(jnp.int32)


def touch_ends(values, stream_key, least, high):
    longest = values.shape.index(max(values.shape))
    spots = []
    for shift in (0, 1):
        where = [jax.random.randint(jax.random.fold_in(stream_key, axis), (), 0, length) for axis, length in enumerate(values.shape)]
        where[longest] = (where[longest] + shift) % values.shape[longest]
        spots.append(tuple(where))
    return values.at[spots[0]].set(least).at[spots[1]].set(high)


def steps_of(key, dims, cuts, least, top_value):
    def one(axis_at, parts):
        steps = jax.random.uniform(jax.random.fold_in(jax.random.fold_in(key, 6), axis_at), (parts,), jnp.float32, least / len(cuts), top_value / len(cuts))
        return jnp.repeat(jnp.exp(steps), dims[axis_at] // parts).reshape((-1,) + (1,) * (len(dims) - axis_at - 1))

    factor_of = one(*cuts[0])
    for cut in cuts[1:]:
        factor_of = factor_of * one(*cut)
    return factor_of


def noise(own_key, shape, scale, most, cuts=(), kind=jnp.bfloat16):
    factor_of = steps_of(own_key, shape, cuts, -0.22, 0.18) if cuts else 1.0
    values = jax.random.normal(own_key, shape, jnp.float32) * scale * factor_of
    return jnp.minimum(jnp.maximum(values, -most), most).astype(kind)


def setup_inputs(seed: int = 0) -> dict:
    arg_keys = jax.random.split(jax.random.key(seed), 15)
    return {
        "positions": draw_positions(jax.random.fold_in(arg_keys[14], 71), 0),
        "forces": noise(arg_keys[1], (3, N_GY, NPS), 1.0, 6.0, ((1, 2), (2, 128)), jnp.float32),
        "deriv_mat": noise(arg_keys[2], (P_SIZE, P_SIZE), P_SIZE ** -0.5, 0.25, (), jnp.float32),
        "quad_mat": noise(arg_keys[3], (P_SIZE, P_SIZE), P_SIZE ** -0.5, 0.25, (), jnp.float32),
        "point_dest": draw_point_dest(jax.random.fold_in(arg_keys[14], 71), 0),
        "leaf_center": draw_leaf_center(jax.random.fold_in(arg_keys[14], 71), 0),
        "tile_src": draw_tile_src(jax.random.fold_in(arg_keys[14], 71), 0),
        "neighbours": draw_neighbours(jax.random.fold_in(arg_keys[14], 71), 0),
        "inter_leaf": draw_inter_leaf(jax.random.fold_in(arg_keys[14], 71), 0),
        "inter_op": touch_ends(jax.random.randint(arg_keys[9], (N_GY, K_IL, NLS), 0, NOPS), jax.random.fold_in(arg_keys[9], 1), 0, NOPS - 1).astype(jnp.int32),
        "coarse_op": draw_coarse_op(jax.random.fold_in(arg_keys[14], 71), 0),
        "up_pinv": noise(arg_keys[11], (EXP, EXP), EXP ** -0.5, 0.5, (), jnp.float32),
        "trans_ops": noise(arg_keys[12], (NOPS, EXP, EXP), (3 * EXP) ** -0.5, 0.25, (), jnp.float32),
        "child_ops": noise(arg_keys[13], (8, EXP, EXP), (EXP * L_DEV) ** -0.5, 0.03125, (), jnp.float32),
    }


SOFTENING = 0.25
RADIUS = 2.5
HIGHEST = lax.Precision.HIGHEST

def sphere_points(count):
    index = jnp.arange(count).astype(jnp.float32)
    height = 1.0 - (2.0 * index + 1.0) / count
    radial = jnp.sqrt(1.0 - height * height)
    angle = 2.399963 * index
    return jnp.stack([radial * jnp.cos(angle), radial * jnp.sin(angle), height])

def stokes_sum(targets, sources, strengths):
    delta_x = targets[0][:, :, None] - sources[0][:, None, :]
    delta_y = targets[1][:, :, None] - sources[1][:, None, :]
    delta_z = targets[2][:, :, None] - sources[2][:, None, :]
    soft_sq = delta_x * delta_x + delta_y * delta_y + delta_z * delta_z + SOFTENING
    inverse = 1.0 / (soft_sq * jnp.sqrt(soft_sq))
    push_x = strengths[0][:, None, :]
    push_y = strengths[1][:, None, :]
    push_z = strengths[2][:, None, :]
    projected = (push_x * delta_x + push_y * delta_y + push_z * delta_z) * inverse
    direct = (soft_sq + SOFTENING) * inverse
    return jnp.stack([lax.optimization_barrier(jnp.sum(push_x * direct + projected * delta_x, axis=2)), lax.optimization_barrier(jnp.sum(push_y * direct + projected * delta_y, axis=2)), lax.optimization_barrier(jnp.sum(push_z * direct + projected * delta_z, axis=2))])

def by_blocks(func, arrays, total, width):

    def one_block(start):
        return func(*[lax.dynamic_slice_in_dim(item, start, width, 1) for item in arrays])
    starts = (jnp.arange(total // width) * width).astype(jnp.int32)
    result = lax.map(one_block, starts)
    return jnp.transpose(result, (1, 0, 2, 3)).reshape(result.shape[1], total, result.shape[3])

def moments(tiles, centers, sphere, up_pinv, width):
    total = centers.shape[1]
    checks = centers[:, :, None] + RADIUS * sphere[:, None, :]
    values = by_blocks(stokes_sum, [checks, tiles[:3], tiles[3:]], total, width)
    stacked = jnp.transpose(values, (0, 2, 1)).reshape(-1, total)
    return jnp.dot(up_pinv.T, stacked, precision=HIGHEST, preferred_element_type=jnp.float32)

def children(multipole, child_ops):
    expansion = multipole.shape[0]
    grouped = lax.optimization_barrier(jnp.sum(multipole.reshape(expansion, -1, L_DEV // 8, 8), axis=2))
    return jnp.einsum('cef,ebc->bf', child_ops, grouped, precision=HIGHEST)

def coarse_terms(op_rows, coarse):
    onehot = (op_rows[:, :, None] == jnp.arange(NOPS)[None, None, :]).astype(jnp.float32)
    return jnp.einsum('tbk,be->tke', onehot, coarse, precision=HIGHEST)

def translate(trans_ops, grouped):
    return jnp.einsum('kef,tke->tf', trans_ops, grouped, precision=HIGHEST)

def leaf_translate(extended, index, op_rows, trans_ops):
    picked = extended[:, index]
    onehot = (op_rows[:, :, None] == jnp.arange(NOPS)[None, None, :]).astype(jnp.float32)
    grouped = jnp.einsum('ejn,jnk->ken', picked, onehot, precision=HIGHEST)
    return jnp.einsum('kef,ken->fn', trans_ops, grouped, precision=HIGHEST)

def downward(coarse_local, child_ops, leaves):
    pushed = jnp.einsum('cfe,be->fbc', child_ops, coarse_local, precision=HIGHEST)
    expansion = pushed.shape[0]
    boxes = pushed.shape[1]
    spread = jnp.broadcast_to(pushed[:, :, None, :], (expansion, boxes, leaves // 8, 8))
    return spread.reshape(expansion, boxes * leaves)

def evaluate(tiles, centers, sphere, local, width):
    total = centers.shape[1]
    surface = centers[:, :, None] + RADIUS * sphere[:, None, :]
    density = jnp.transpose(local.reshape(3, -1, total), (0, 2, 1))
    return by_blocks(stokes_sum, [tiles[:3], surface, density], total, width)

def route(packed_slab, dest, table):
    source = packed_slab.reshape(6, N_GX, NPD)

    def fill(data, where):
        return jnp.zeros((6, N_GX * CAP), jnp.float32).at[:, where].set(data)
    sent = jax.vmap(fill, in_axes=(1, 0), out_axes=1)(source, dest.reshape(N_GX, NPD))
    sent = sent.reshape(6, N_GX, N_GX, CAP)
    received = jnp.transpose(sent, (0, 2, 1, 3)).reshape(6, N_GX, N_GX * CAP)
    received = jnp.concatenate([received, jnp.zeros((6, N_GX, 1), jnp.float32)], axis=2)
    rows = table.reshape(N_GX, L_DEV * TILE)
    tiles = jnp.take_along_axis(received, jnp.broadcast_to(rows[None], (6,) + rows.shape), axis=2)
    return tiles.reshape(6, NLS, TILE)

def unroute(flow, dest, table):
    rows = table.reshape(N_GX, L_DEV * TILE)
    per_owner = flow.reshape(3, N_GX, L_DEV * TILE)

    def place(values, where):
        return jnp.zeros((3, N_GX * CAP + 1), jnp.float32).at[:, where].set(values)[:, :N_GX * CAP]
    back = jax.vmap(place, in_axes=(1, 0), out_axes=1)(per_owner, rows)
    back = jnp.transpose(back.reshape(3, N_GX, N_GX, CAP), (0, 2, 1, 3)).reshape(3, N_GX, N_GX * CAP)
    where = dest.reshape(N_GX, NPD)
    points = jnp.take_along_axis(back, jnp.broadcast_to(where[None], (3,) + where.shape), axis=2)
    return points.reshape(3, NPS)

def reference(positions, forces, deriv_mat, quad_mat, point_dest, leaf_center, tile_src, neighbours, inter_leaf, inter_op, coarse_op, up_pinv, trans_ops, child_ops):
    tangent = jnp.dot(positions.reshape(-1, P_SIZE), deriv_mat, precision=HIGHEST, preferred_element_type=jnp.float32).reshape(positions.shape)
    jacobian = jnp.sqrt(1.0 + lax.optimization_barrier(jnp.sum(tangent * tangent, axis=0)))
    weighted = jnp.dot(forces.reshape(-1, P_SIZE), quad_mat, precision=HIGHEST, preferred_element_type=jnp.float32).reshape(forces.shape)
    packed = jnp.concatenate([positions, weighted * jacobian[None]], axis=0)
    sphere = sphere_points(SURF)
    width = 64
    tile_sets = []
    multipoles = []
    for slab in range(N_GY):
        tiles = route(packed[:, slab], point_dest[slab], tile_src[slab])
        tile_sets.append(tiles)
        multipoles.append(moments(tiles, leaf_center[:, slab], sphere, up_pinv, width))
    coarse = jnp.stack([children(item, child_ops) for item in multipoles], axis=1).reshape(-1, EXP)
    outputs = []
    for slab in range(N_GY):
        tiles = tile_sets[slab]
        picked = tiles[:, neighbours[slab].T].reshape(6, NLS, -1)
        near = by_blocks(stokes_sum, [tiles[:3], picked[:3], picked[3:]], NLS, width)
        local = leaf_translate(multipoles[slab], inter_leaf[slab], inter_op[slab], trans_ops)
        coarse_local = translate(trans_ops, coarse_terms(coarse_op[slab], coarse))
        local = local + downward(coarse_local, child_ops, L_DEV)
        far = evaluate(tiles, leaf_center[:, slab], sphere, local, width)
        flow = ((near + far) / (8.0 * math.pi)).reshape(3, -1)
        outputs.append(unroute(flow, point_dest[slab], tile_src[slab]))
    return jnp.stack(outputs, axis=1)
```

```python
import functools
import math

import jax
import jax.numpy as jnp
from jax import lax
from jax.experimental import pallas as pl
from jax.experimental.pallas import tpu as pltpu
from jax.sharding import PartitionSpec as P

P_SIZE = 544
NOPS = 16
TILE = 128
LANES = 128
SURF = 56
SURF_PAD = 64
SOFTENING = 0.25
RADIUS = 2.5
HIGHEST = lax.Precision.HIGHEST
F32 = jnp.float32
BF16 = jnp.bfloat16

VMEM = pl.BlockSpec(memory_space=pltpu.VMEM)
SMEM = pl.BlockSpec(memory_space=pltpu.SMEM)


def params():
    return pltpu.CompilerParams(vmem_limit_bytes=60 * 1024 * 1024)


def sphere_points(count):
    index = jnp.arange(count).astype(F32)
    height = 1.0 - (2.0 * index + 1.0) / count
    radial = jnp.sqrt(1.0 - height * height)
    angle = 2.399963 * index
    return jnp.stack([radial * jnp.cos(angle), radial * jnp.sin(angle), height])


def aligned(index, step):
    return pl.multiple_of(index * step, step)


def split_bf16(value):
    high = value.astype(BF16)
    low = (value - high.astype(F32)).astype(BF16)
    return high, low


def dot_nt(left, right):
    return lax.dot_general(left, right, (((1,), (1,)), ((), ())), preferred_element_type=F32)


def dot_nn(left, right):
    return lax.dot_general(left, right, (((1,), (0,)), ((), ())), preferred_element_type=F32)


def move_rows(write, indices, block):
    part = indices.at[pl.ds(block * TILE, TILE)]
    for row in range(TILE):
        write(row, part[row])


def to_rows_table(source, table, blocks, width):
    def one(block, carry):
        rows = source[pl.ds(block * width, width), :]
        table[pl.ds(aligned(block, TILE), TILE), 0:width] = rows.T
        return carry

    lax.fori_loop(0, blocks, one, 0, unroll=4)


def from_rows_table(table, out, blocks, width):
    def one(block, carry):
        rows = table[pl.ds(aligned(block, TILE), TILE), 0:8].T
        out[pl.ds(block * width, width), :] = rows[0:width]
        return carry

    lax.fori_loop(0, blocks, one, 0, unroll=4)


def send_kernel(dest, packed, out, table, stage):
    blocks = packed.shape[1] // LANES

    def one(block, carry):
        stage[:, 0:8] = packed[:, pl.ds(aligned(block, LANES), LANES)].T

        def write(row, index):
            table[pl.ds(index, 1), :] = stage[pl.ds(row, 1), :]

        move_rows(write, dest, block)
        return carry

    lax.fori_loop(0, blocks, one, 0)
    from_rows_table(table, out, out.shape[0] // 6, 6)


def features(x_rows, g_rows, store_a, store_d):
    gdotx = g_rows[0] * x_rows[0] + g_rows[1] * x_rows[1] + g_rows[2] * x_rows[2]
    for c in range(3):
        store_d(c, g_rows[c])
        store_a(c, gdotx * x_rows[c])
    for k in range(3):
        for c in range(3):
            store_a(3 + 3 * k + c, g_rows[k] * x_rows[c])
    for k in range(3):
        store_a(12 + k, g_rows[k])
    store_a(15, gdotx)


def combine(sums, y_rows):
    along = (
        y_rows[0] * sums[12:13] + y_rows[1] * sums[13:14] + y_rows[2] * sums[14:15] - sums[15:16]
    )
    flows = []
    for c in range(3):
        crossed = y_rows[0] * sums[3 + c : 4 + c]
        crossed = crossed + y_rows[1] * sums[6 + c : 7 + c]
        crossed = crossed + y_rows[2] * sums[9 + c : 10 + c]
        flows.append(sums[c : c + 1] + y_rows[c] * along - crossed)
    return flows


def pair_weights(dx, dy, dz):
    soft_sq = (dx * dx + dy * dy) + (dz * dz + SOFTENING)
    root = lax.rsqrt(soft_sq)
    cube = root * root * root
    return cube, root + SOFTENING * cube


def receive_kernel(source, centers, arrived, surface, surf_rows, tiles, checks, table, stage, feat):
    leaves = tiles.shape[0] // 6
    slots = leaves * TILE
    to_rows_table(arrived, table, slots // TILE, 6)
    table[pl.ds(slots, 8), :] = jnp.zeros((8, LANES), F32)
    feat[...] = jnp.zeros(feat.shape, F32)

    def gather(leaf, slot):
        def write(row, index):
            stage[pl.ds(slot * TILE + row, 1), :] = table[pl.ds(index, 1), :]

        move_rows(write, source, leaf)

    def check(leaf, slot):
        rows = stage[slot * TILE : slot * TILE + TILE, 0:8].T
        tiles[pl.ds(leaf * 6, 6), :] = rows[0:6]
        x_rows = [rows[c : c + 1] - centers[c * leaves + leaf] for c in range(3)]
        g_rows = [rows[3 + c : 4 + c] for c in range(3)]

        def store_a(row, value):
            feat[slot * 32 + row : slot * 32 + row + 1, :] = value

        def store_d(row, value):
            feat[slot * 32 + 16 + row : slot * 32 + 17 + row, :] = value

        features(x_rows, g_rows, store_a, store_d)
        both = feat[slot * 32 : slot * 32 + 32, :]
        high, low = split_bf16(both)
        cube, direct = pair_weights(
            surface[0] - x_rows[0], surface[1] - x_rows[1], surface[2] - x_rows[2]
        )
        cube_high, cube_low = split_bf16(cube)
        dir_high, dir_low = split_bf16(direct)
        sums = dot_nt(high[0:16], cube_high) + dot_nt(high[0:16], cube_low)
        sums = sums + dot_nt(low[0:16], cube_high) + dot_nt(high[16:32], dir_high)
        sums = sums + dot_nt(high[16:32], dir_low) + dot_nt(low[16:32], dir_high)
        flows = combine(sums, [surf_rows[c : c + 1, 0:SURF_PAD] for c in range(3)])
        for c in range(3):
            checks[pl.ds(leaf * 3 + c, 1), 0:SURF_PAD] = flows[c]

    gather(0, 0)

    def pair(step, carry):
        leaf = step * 2
        gather(leaf + 1, 1)
        check(leaf, 0)
        gather(jnp.minimum(leaf + 2, leaves - 1), 0)
        check(leaf + 1, 1)
        return carry

    lax.fori_loop(0, leaves // 2, pair, 0)


def near_kernel(listed, places, centers, own, extended, *rest):
    before = rest[0] if len(rest) == 3 else None
    out, target = rest[-2:]
    leaves = own.shape[0] // 6

    def one(leaf, carry):
        shift = [centers[c * leaves + leaf] for c in range(3)]
        rows = own[pl.ds(leaf * 6, 6), :]
        target[:, 0:6] = rows.T
        y_rows = [own[pl.ds(leaf * 6 + c, 1), :] - shift[c] for c in range(3)]
        left_d, left_w, sources = [], [], []
        for n in range(listed):
            place = places[n * leaves + leaf] * 6
            tile = [extended[pl.ds(place + c, 1), :] for c in range(6)]
            sources.append([jnp.broadcast_to(row, (8, LANES)) for row in tile])
            grow = [split_bf16(tile[3 + c]) for c in range(3)]
            xrow = [split_bf16(tile[c] - shift[c]) for c in range(3)]
            ones = jnp.ones((1, LANES), BF16)
            zero = jnp.zeros((1, LANES), BF16)
            left_d.append(jnp.concatenate([g[0] for g in grow] + [g[1] for g in grow] + [zero] * 10))
            left_w.append(
                jnp.concatenate([x[0] for x in xrow] + [x[1] for x in xrow] + [ones] + [zero] * 9)
            )
        sum_d = jnp.zeros((16, TILE), F32)
        sum_w = jnp.zeros((16, TILE), F32)
        sum_dl = jnp.zeros((16, TILE), F32)
        sum_wl = jnp.zeros((16, TILE), F32)
        directs = [[] for _ in range(listed)]
        pushes = [[] for _ in range(listed)]
        for block in range(TILE // 8):
            y = [
                jnp.broadcast_to(target[8 * block : 8 * block + 8, c : c + 1], (8, LANES))
                for c in range(3)
            ]
            for n in range(listed):
                x = sources[n]
                dx, dy, dz = y[0] - x[0], y[1] - x[1], y[2] - x[2]
                cube, direct = pair_weights(dx, dy, dz)
                directs[n].append(direct)
                pushes[n].append(cube * ((x[3] * dx + x[4] * dy) + x[5] * dz))
        for n in range(listed):
            dir_high, dir_low = split_bf16(jnp.concatenate(directs[n]))
            push_high, push_low = split_bf16(jnp.concatenate(pushes[n]))
            sum_d = sum_d + dot_nt(left_d[n], dir_high)
            sum_dl = sum_dl + dot_nt(left_d[n], dir_low)
            sum_w = sum_w + dot_nt(left_w[n], push_high)
            sum_wl = sum_wl + dot_nt(left_w[n], push_low)
        whole = sum_w[6:7] + sum_wl[6:7]
        for c in range(3):
            direct = sum_d[c : c + 1] + sum_d[3 + c : 4 + c] + sum_dl[c : c + 1]
            moved = sum_w[c : c + 1] + sum_w[3 + c : 4 + c] + sum_wl[c : c + 1]
            total = direct + (y_rows[c] * whole - moved)
            if before is not None:
                total = total + before[pl.ds(leaf * 3 + c, 1), :]
            out[pl.ds(leaf * 3 + c, 1), :] = total
        return carry

    lax.fori_loop(0, leaves, one, 0)


def far_kernel(source, centers, own, near, local, surface, surf_rows, out, table, stage, feat):
    leaves = own.shape[0] // 6
    scale = 1.0 / (8.0 * math.pi)
    feat[...] = jnp.zeros(feat.shape, F32)
    stage[...] = jnp.zeros(stage.shape, F32)

    def scatter(leaf, slot):
        def write(row, index):
            table[pl.ds(index, 1), :] = stage[pl.ds(slot * TILE + row, 1), :]

        move_rows(write, source, leaf)

    def far(leaf, slot):
        y_rows = [own[pl.ds(leaf * 6 + c, 1), :] - centers[c * leaves + leaf] for c in range(3)]
        g_rows = [local[pl.ds(leaf * 3 + c, 1), :] for c in range(3)]
        x_rows = [surf_rows[c : c + 1, :] for c in range(3)]

        def store_a(row, value):
            feat[slot * 32 + row : slot * 32 + row + 1, :] = value

        def store_d(row, value):
            feat[slot * 32 + 16 + row : slot * 32 + 17 + row, :] = value

        features(x_rows, g_rows, store_a, store_d)
        both = feat[slot * 32 : slot * 32 + 32, 0:SURF_PAD]
        high, low = split_bf16(both)
        cube, direct = pair_weights(
            y_rows[0] - surface[0], y_rows[1] - surface[1], y_rows[2] - surface[2]
        )
        cube_high, cube_low = split_bf16(cube)
        dir_high, dir_low = split_bf16(direct)
        sums = dot_nn(high[0:16], cube_high) + dot_nn(high[0:16], cube_low)
        sums = sums + dot_nn(low[0:16], cube_high) + dot_nn(high[16:32], dir_high)
        sums = sums + dot_nn(high[16:32], dir_low) + dot_nn(low[16:32], dir_high)
        flows = combine(sums, y_rows)
        total = [(flows[c] + near[pl.ds(leaf * 3 + c, 1), :]) * scale for c in range(3)]
        for c in range(3):
            feat[64 + slot * 8 + c : 65 + slot * 8 + c, :] = total[c]
        stage[slot * TILE : slot * TILE + TILE, 0:8] = feat[64 + slot * 8 : 72 + slot * 8, :].T

    far(0, 0)

    def pair(step, carry):
        leaf = step * 2
        far(leaf + 1, 1)
        scatter(leaf, 0)
        far(jnp.minimum(leaf + 2, leaves - 1), 0)
        scatter(leaf + 1, 1)
        return carry

    lax.fori_loop(0, leaves // 2, pair, 0)
    from_rows_table(table, out, out.shape[0] // 3, 3)


def return_kernel(dest, arrived, out, table, stage):
    to_rows_table(arrived, table, arrived.shape[0] // 3, 3)

    def one(block, carry):
        def write(row, index):
            stage[pl.ds(row, 1), :] = table[pl.ds(index, 1), :]

        move_rows(write, dest, block)
        out[:, pl.ds(aligned(block, LANES), LANES)] = stage[:, 0:8].T
        return carry

    lax.fori_loop(0, out.shape[1] // LANES, one, 0)


def exchange(rows, owners):
    blocks = rows.reshape(owners, 1, -1)
    blocks = lax.all_to_all(blocks, "gx", split_axis=0, concat_axis=0, tiled=True)
    return blocks.reshape(rows.shape)


def near_sum(listed, places, centers, tiles, extended, before):
    return pl.pallas_call(
        functools.partial(near_kernel, listed),
        out_shape=jax.ShapeDtypeStruct((tiles.shape[0] // 2, LANES), F32),
        in_specs=[SMEM, SMEM, VMEM, VMEM] + [VMEM] * len(before),
        out_specs=VMEM,
        scratch_shapes=[pltpu.VMEM((TILE, LANES), F32)],
        compiler_params=params(),
        cost_estimate=pl.CostEstimate(
            flops=listed * 10**10, transcendentals=0, bytes_accessed=10**7
        ),
        name=f"near{listed}",
    )(places, centers, tiles, extended, *before)


def halo(shard, devices):
    up = [(i, i + 1) for i in range(devices - 1)]
    down = [(i + 1, i) for i in range(devices - 1)]
    before = lax.ppermute(shard, "gx", up)
    after = lax.ppermute(shard, "gx", down)
    return jnp.concatenate([before, shard, after], axis=0)


def body(
    positions,
    forces,
    deriv_mat,
    quad_mat,
    point_dest,
    leaf_center,
    tile_src,
    neighbours,
    inter_leaf,
    inter_op,
    coarse_op,
    up_pinv,
    trans_ops,
    child_ops,
):
    owners = lax.axis_size("gx")
    count = positions.shape[2]
    leaves = leaf_center.shape[2]
    slots = leaves * TILE
    expansion = up_pinv.shape[0]
    shape = jax.ShapeDtypeStruct
    first = lax.axis_index("gx") * leaves - leaves

    tangent = jnp.dot(
        positions.reshape(-1, P_SIZE), deriv_mat, precision=HIGHEST, preferred_element_type=F32
    ).reshape(3, count)
    jacobian = jnp.sqrt(1.0 + jnp.sum(tangent * tangent, axis=0))
    weighted = jnp.dot(
        forces.reshape(-1, P_SIZE), quad_mat, precision=HIGHEST, preferred_element_type=F32
    ).reshape(3, count)
    packed = jnp.concatenate(
        [positions.reshape(3, count), weighted * jacobian[None], jnp.zeros((2, count), F32)], axis=0
    )
    outgoing = pl.pallas_call(
        send_kernel,
        out_shape=shape((6 * slots // LANES, LANES), F32),
        in_specs=[SMEM, VMEM],
        out_specs=VMEM,
        scratch_shapes=[pltpu.VMEM((slots, LANES), F32), pltpu.VMEM((TILE, LANES), F32)],
        compiler_params=params(),
        name="send",
    )(point_dest.reshape(count), packed)
    arrived = exchange(outgoing, owners)

    source = tile_src.reshape(slots)
    centers = leaf_center.reshape(3 * leaves)
    sphere = RADIUS * sphere_points(SURF)
    surf_rows = jnp.pad(sphere, ((0, 5), (0, LANES - SURF)))
    surface = jnp.broadcast_to(surf_rows[:3, :SURF_PAD, None], (3, SURF_PAD, LANES))
    tiles, checks = pl.pallas_call(
        receive_kernel,
        out_shape=[shape((6 * leaves, LANES), F32), shape((3 * leaves, LANES), F32)],
        in_specs=[SMEM, SMEM, VMEM, VMEM, VMEM],
        out_specs=[VMEM, VMEM],
        scratch_shapes=[
            pltpu.VMEM((slots + 8, LANES), F32),
            pltpu.VMEM((2 * TILE, LANES), F32),
            pltpu.VMEM((64, LANES), F32),
        ],
        compiler_params=params(),
        name="receive",
    )(source, centers, arrived, surface, surf_rows)

    extended = halo(tiles, owners)
    check = checks.reshape(leaves, 3, LANES)[:, :, :SURF].reshape(leaves, expansion)
    multipole = jnp.dot(check, up_pinv, precision=HIGHEST, preferred_element_type=F32)
    multipole_ext = halo(multipole, owners)
    grouped = jnp.sum(multipole.reshape(leaves // 8, 8, expansion), axis=0)
    moment = jnp.einsum("ce,cef->f", grouped, child_ops, precision=HIGHEST)
    moment = jnp.pad(moment, (0, 8 * LANES - expansion)).reshape(8, LANES)
    coarse = lax.all_gather(moment, ("gx", "gy"), axis=0, tiled=True)

    near = near_sum(1, jnp.arange(leaves), centers, tiles, tiles, [])
    places = (neighbours[0, 1:] - first).reshape(2 * leaves)
    near = near_sum(2, places, centers, tiles, extended, [near])

    near, coarse, multipole_ext = lax.optimization_barrier((near, coarse, multipole_ext))
    coarse = coarse.reshape(-1, 8, LANES)[:, :2].reshape(-1, 2 * LANES)[:, :expansion]
    op_ids = jnp.arange(NOPS)
    onehot = (coarse_op[0, 0][:, None] == op_ids[None, :]).astype(F32)
    by_op = jnp.einsum("bk,be->ke", onehot, coarse, precision=HIGHEST)
    coarse_local = jnp.einsum("ke,kef->f", by_op, trans_ops, precision=HIGHEST)
    pushed = jnp.einsum("cfe,e->cf", child_ops, coarse_local, precision=HIGHEST)

    picked = jnp.take(multipole_ext, (inter_leaf[0] - first).T, axis=0)
    leaf_hot = (inter_op[0].T[:, :, None] == op_ids[None, None, :]).astype(F32)
    leaf_by_op = jnp.einsum("nje,njk->nke", picked, leaf_hot, precision=HIGHEST)
    local = jnp.dot(
        leaf_by_op.reshape(leaves, NOPS * expansion),
        trans_ops.reshape(NOPS * expansion, expansion),
        precision=HIGHEST,
        preferred_element_type=F32,
    )
    local = (local.reshape(leaves // 8, 8, expansion) + pushed[None]).reshape(leaves, 3, SURF)
    local = jnp.pad(local, ((0, 0), (0, 0), (0, LANES - SURF))).reshape(3 * leaves, LANES)

    returning = pl.pallas_call(
        far_kernel,
        out_shape=shape((3 * slots // LANES, LANES), F32),
        in_specs=[SMEM, SMEM, VMEM, VMEM, VMEM, VMEM, VMEM],
        out_specs=VMEM,
        scratch_shapes=[
            pltpu.VMEM((slots + 8, LANES), F32),
            pltpu.VMEM((2 * TILE, LANES), F32),
            pltpu.VMEM((80, LANES), F32),
        ],
        compiler_params=params(),
        name="far",
    )(source, centers, tiles, near, local, surface, surf_rows)
    came_back = exchange(returning, owners)
    velocity = pl.pallas_call(
        return_kernel,
        out_shape=shape((8, count), F32),
        in_specs=[SMEM, VMEM],
        out_specs=VMEM,
        scratch_shapes=[pltpu.VMEM((slots, LANES), F32), pltpu.VMEM((TILE, LANES), F32)],
        compiler_params=params(),
        name="back",
    )(point_dest.reshape(count), came_back)
    return velocity[:3].reshape(3, 1, count)


def solution(mesh):
    in_specs = (
        P(None, "gy", "gx"),
        P(None, "gy", "gx"),
        P(),
        P(),
        P("gy", "gx"),
        P(None, "gy", "gx"),
        P("gy", "gx"),
        P("gy", None, "gx"),
        P("gy", None, "gx"),
        P("gy", None, "gx"),
        P("gy", "gx", None),
        P(),
        P(),
        P(),
    )
    out_specs = P(None, "gy", "gx")
    return jax.shard_map(body, mesh=mesh, in_specs=in_specs, out_specs=out_specs, check_vma=False)
```

```python
import functools
import math

import jax
import jax.numpy as jnp
from jax import lax
from jax.experimental import pallas as pl
from jax.experimental.pallas import tpu as pltpu
from jax.sharding import PartitionSpec as P

P_SIZE = 544
NOPS = 16
TILE = 128
LANES = 128
SURF = 56
SURF_PAD = 64
SOFTENING = 0.25
RADIUS = 2.5
HIGHEST = lax.Precision.HIGHEST
F32 = jnp.float32
BF16 = jnp.bfloat16

VMEM = pl.BlockSpec(memory_space=pltpu.VMEM)
SMEM = pl.BlockSpec(memory_space=pltpu.SMEM)


def params():
    return pltpu.CompilerParams(vmem_limit_bytes=60 * 1024 * 1024)


def sphere_points(count):
    index = jnp.arange(count).astype(F32)
    height = 1.0 - (2.0 * index + 1.0) / count
    radial = jnp.sqrt(1.0 - height * height)
    angle = 2.399963 * index
    return jnp.stack([radial * jnp.cos(angle), radial * jnp.sin(angle), height])


def aligned(index, step):
    return pl.multiple_of(index * step, step)


def split_bf16(value):
    high = value.astype(BF16)
    low = (value - high.astype(F32)).astype(BF16)
    return high, low


def dot_nt(left, right):
    return lax.dot_general(left, right, (((1,), (1,)), ((), ())), preferred_element_type=F32)


def dot_nn(left, right):
    return lax.dot_general(left, right, (((1,), (0,)), ((), ())), preferred_element_type=F32)


def move_rows(write, indices, block):
    part = indices.at[pl.ds(block * TILE, TILE)]
    for row in range(TILE):
        write(row, part[row])


def to_rows_table(source, table, blocks, width):
    def one(block, carry):
        rows = source[pl.ds(block * width, width), :]
        table[pl.ds(aligned(block, TILE), TILE), 0:width] = rows.T
        return carry

    lax.fori_loop(0, blocks, one, 0, unroll=4)


def from_rows_table(table, out, blocks, width):
    def one(block, carry):
        rows = table[pl.ds(aligned(block, TILE), TILE), 0:8].T
        out[pl.ds(block * width, width), :] = rows[0:width]
        return carry

    lax.fori_loop(0, blocks, one, 0, unroll=4)


def send_kernel(dest, packed, out, table, stage):
    blocks = packed.shape[1] // LANES

    def one(block, carry):
        stage[:, 0:8] = packed[:, pl.ds(aligned(block, LANES), LANES)].T

        def write(row, index):
            table[pl.ds(index, 1), :] = stage[pl.ds(row, 1), :]

        move_rows(write, dest, block)
        return carry

    lax.fori_loop(0, blocks, one, 0)
    from_rows_table(table, out, out.shape[0] // 6, 6)


def features(x_rows, g_rows, store_a, store_d):
    gdotx = g_rows[0] * x_rows[0] + g_rows[1] * x_rows[1] + g_rows[2] * x_rows[2]
    for c in range(3):
        store_d(c, g_rows[c])
        store_a(c, gdotx * x_rows[c])
    for k in range(3):
        for c in range(3):
            store_a(3 + 3 * k + c, g_rows[k] * x_rows[c])
    for k in range(3):
        store_a(12 + k, g_rows[k])
    store_a(15, gdotx)


def combine(sums, y_rows):
    along = (
        y_rows[0] * sums[12:13] + y_rows[1] * sums[13:14] + y_rows[2] * sums[14:15] - sums[15:16]
    )
    flows = []
    for c in range(3):
        crossed = y_rows[0] * sums[3 + c : 4 + c]
        crossed = crossed + y_rows[1] * sums[6 + c : 7 + c]
        crossed = crossed + y_rows[2] * sums[9 + c : 10 + c]
        flows.append(sums[c : c + 1] + y_rows[c] * along - crossed)
    return flows


def pair_weights(dx, dy, dz):
    soft_sq = (dx * dx + dy * dy) + (dz * dz + SOFTENING)
    root = lax.rsqrt(soft_sq)
    cube = root * root * root
    return cube, root + SOFTENING * cube


def receive_kernel(source, centers, arrived, surface, surf_rows, tiles, checks, table, stage, feat):
    leaves = tiles.shape[0] // 8
    slots = leaves * TILE
    to_rows_table(arrived, table, slots // TILE, 6)
    table[pl.ds(slots, 8), :] = jnp.zeros((8, LANES), F32)
    feat[...] = jnp.zeros(feat.shape, F32)

    def gather(leaf, slot):
        def write(row, index):
            stage[pl.ds(slot * TILE + row, 1), :] = table[pl.ds(index, 1), :]

        move_rows(write, source, leaf)

    def check(leaf, slot):
        rows = stage[slot * TILE : slot * TILE + TILE, 0:8].T
        at = [rows[c : c + 1] for c in range(6)]
        size = at[0] * at[0] + at[1] * at[1] + at[2] * at[2] + 0.5 * SOFTENING
        along = at[0] * at[3] + at[1] * at[4] + at[2] * at[5]
        tiles[pl.ds(aligned(leaf, 8), 8), :] = jnp.concatenate([rows[0:6], size, -along])
        x_rows = [rows[c : c + 1] - centers[c * leaves + leaf] for c in range(3)]
        g_rows = [rows[3 + c : 4 + c] for c in range(3)]

        def store_a(row, value):
            feat[slot * 32 + row : slot * 32 + row + 1, :] = value

        def store_d(row, value):
            feat[slot * 32 + 16 + row : slot * 32 + 17 + row, :] = value

        features(x_rows, g_rows, store_a, store_d)
        both = feat[slot * 32 : slot * 32 + 32, :]
        high, low = split_bf16(both)
        cube, direct = pair_weights(
            surface[0] - x_rows[0], surface[1] - x_rows[1], surface[2] - x_rows[2]
        )
        cube_high, cube_low = split_bf16(cube)
        dir_high, dir_low = split_bf16(direct)
        sums = dot_nt(high[0:16], cube_high) + dot_nt(high[0:16], cube_low)
        sums = sums + dot_nt(low[0:16], cube_high) + dot_nt(high[16:32], dir_high)
        sums = sums + dot_nt(high[16:32], dir_low) + dot_nt(low[16:32], dir_high)
        flows = combine(sums, [surf_rows[c : c + 1, 0:SURF_PAD] for c in range(3)])
        for c in range(3):
            checks[pl.ds(leaf * 3 + c, 1), 0:SURF_PAD] = flows[c]

    gather(0, 0)

    def pair(step, carry):
        leaf = step * 2
        gather(leaf + 1, 1)
        check(leaf, 0)
        gather(jnp.minimum(leaf + 2, leaves - 1), 0)
        check(leaf + 1, 1)
        return carry

    lax.fori_loop(0, leaves // 2, pair, 0)


def triple_split(value):
    first = value.astype(BF16).astype(F32)
    rest = value - first
    second = rest.astype(BF16).astype(F32)
    return first, second, (rest - second).astype(BF16).astype(F32)


def row_at(value, row):
    return jnp.broadcast_to(value[row : row + 1], (8, LANES))


def near_kernel(listed, places, own, extended, *rest):
    before = rest[0] if len(rest) == 2 else None
    out = rest[-1]
    leaves = own.shape[0] // 8
    row = lax.broadcasted_iota(jnp.int32, (8, LANES), 0)
    zero = jnp.zeros((8, LANES), F32)
    one_row = jnp.ones((8, LANES), F32)

    def one(leaf, carry):
        mine = own[pl.ds(aligned(leaf, 8), 8), :]
        parts = triple_split(mine)
        dist, push = [], []
        for part in parts:
            dist.append(jnp.where(row < 3, -2.0 * part, zero))
            turned = pltpu.roll(part, 3, 0)
            push.append(jnp.where((row >= 3) & (row < 6), turned, zero))
        dist_one = jnp.where(row == 6, 1.0, dist[0])
        push_one = jnp.where(row == 7, 1.0, push[0])
        squares = jnp.where(row == 0, row_at(parts[0], 6), zero)
        squares = jnp.where(row == 1, row_at(parts[1], 6), squares)
        squares = jnp.where(row == 2, row_at(parts[2], 6), squares)
        left = [dist_one] * 3 + [dist[1]] * 2 + [dist[2], squares, zero]
        right = [push_one] * 3 + [push[1]] * 2 + [push[2], zero, zero]
        targets = jnp.concatenate(
            [jnp.concatenate(left).astype(BF16), jnp.concatenate(right).astype(BF16)], axis=1
        )
        sums = jnp.zeros((16, 2 * LANES), F32)
        for n in range(listed):
            tile = extended[pl.ds(aligned(places[n * leaves + leaf], 8), 8), :]
            high, mid, low = triple_split(tile)
            sources = jnp.concatenate([high, mid, low, high, mid, high, one_row, zero]).astype(BF16)
            pairs = lax.dot_general(
                sources, targets, (((0,), (0,)), ((), ())), preferred_element_type=F32
            )
            root = lax.rsqrt(pairs[:, :LANES])
            cube = root * root * root
            direct = root + SOFTENING * cube
            both = jnp.concatenate([direct, cube * pairs[:, LANES:]], axis=1)
            both_high, both_low = split_bf16(both)
            weights = jnp.concatenate([jnp.where(row == 6, 1.0, high), jnp.where(row == 6, 0.0, mid)])
            weights = weights.astype(BF16)
            sums = sums + dot_nn(
                jnp.concatenate([weights, weights], axis=1),
                jnp.concatenate([both_high, both_low], axis=0),
            )
        total = sums[0:8] + sums[8:16]
        moved = total[:, LANES:]
        flow = pltpu.roll(total[:, :LANES], 5, 0) + (mine * row_at(moved, 6) - moved)
        if before is not None:
            flow = flow + before[pl.ds(aligned(leaf, 8), 8), :]
        out[pl.ds(aligned(leaf, 8), 8), :] = flow
        return carry

    lax.fori_loop(0, leaves, one, 0, unroll=2)


def far_kernel(source, centers, own, near, local, surface, surf_rows, out, table, stage, feat):
    leaves = own.shape[0] // 8
    scale = 1.0 / (8.0 * math.pi)
    feat[...] = jnp.zeros(feat.shape, F32)
    stage[...] = jnp.zeros(stage.shape, F32)

    def scatter(leaf, slot):
        def write(row, index):
            table[pl.ds(index, 1), :] = stage[pl.ds(slot * TILE + row, 1), :]

        move_rows(write, source, leaf)

    def far(leaf, slot):
        y_rows = [own[pl.ds(leaf * 8 + c, 1), :] - centers[c * leaves + leaf] for c in range(3)]
        g_rows = [local[pl.ds(leaf * 3 + c, 1), :] for c in range(3)]
        x_rows = [surf_rows[c : c + 1, :] for c in range(3)]

        def store_a(row, value):
            feat[slot * 32 + row : slot * 32 + row + 1, :] = value

        def store_d(row, value):
            feat[slot * 32 + 16 + row : slot * 32 + 17 + row, :] = value

        features(x_rows, g_rows, store_a, store_d)
        both = feat[slot * 32 : slot * 32 + 32, 0:SURF_PAD]
        high, low = split_bf16(both)
        cube, direct = pair_weights(
            y_rows[0] - surface[0], y_rows[1] - surface[1], y_rows[2] - surface[2]
        )
        cube_high, cube_low = split_bf16(cube)
        dir_high, dir_low = split_bf16(direct)
        sums = dot_nn(high[0:16], cube_high) + dot_nn(high[0:16], cube_low)
        sums = sums + dot_nn(low[0:16], cube_high) + dot_nn(high[16:32], dir_high)
        sums = sums + dot_nn(high[16:32], dir_low) + dot_nn(low[16:32], dir_high)
        flows = combine(sums, y_rows)
        total = [(flows[c] + near[pl.ds(leaf * 8 + c, 1), :]) * scale for c in range(3)]
        for c in range(3):
            feat[64 + slot * 8 + c : 65 + slot * 8 + c, :] = total[c]
        stage[slot * TILE : slot * TILE + TILE, 0:8] = feat[64 + slot * 8 : 72 + slot * 8, :].T

    far(0, 0)

    def pair(step, carry):
        leaf = step * 2
        far(leaf + 1, 1)
        scatter(leaf, 0)
        far(jnp.minimum(leaf + 2, leaves - 1), 0)
        scatter(leaf + 1, 1)
        return carry

    lax.fori_loop(0, leaves // 2, pair, 0)
    from_rows_table(table, out, out.shape[0] // 3, 3)


def return_kernel(dest, arrived, out, table, stage):
    to_rows_table(arrived, table, arrived.shape[0] // 3, 3)

    def one(block, carry):
        def write(row, index):
            stage[pl.ds(row, 1), :] = table[pl.ds(index, 1), :]

        move_rows(write, dest, block)
        out[:, pl.ds(aligned(block, LANES), LANES)] = stage[:, 0:8].T
        return carry

    lax.fori_loop(0, out.shape[1] // LANES, one, 0)


def exchange(rows, owners):
    blocks = rows.reshape(owners, 1, -1)
    blocks = lax.all_to_all(blocks, "gx", split_axis=0, concat_axis=0, tiled=True)
    return blocks.reshape(rows.shape)


def near_sum(listed, places, tiles, extended, before):
    return pl.pallas_call(
        functools.partial(near_kernel, listed),
        out_shape=jax.ShapeDtypeStruct(tiles.shape, F32),
        in_specs=[SMEM, VMEM, VMEM] + [VMEM] * len(before),
        out_specs=VMEM,
        compiler_params=params(),
        cost_estimate=pl.CostEstimate(
            flops=listed * 10**10, transcendentals=0, bytes_accessed=10**7
        ),
        name=f"near{listed}",
    )(places, tiles, extended, *before)


def halo(shard, devices):
    up = [(i, i + 1) for i in range(devices - 1)]
    down = [(i + 1, i) for i in range(devices - 1)]
    before = lax.ppermute(shard, "gx", up)
    after = lax.ppermute(shard, "gx", down)
    return jnp.concatenate([before, shard, after], axis=0)


def body(
    positions,
    forces,
    deriv_mat,
    quad_mat,
    point_dest,
    leaf_center,
    tile_src,
    neighbours,
    inter_leaf,
    inter_op,
    coarse_op,
    up_pinv,
    trans_ops,
    child_ops,
):
    owners = lax.axis_size("gx")
    count = positions.shape[2]
    leaves = leaf_center.shape[2]
    slots = leaves * TILE
    expansion = up_pinv.shape[0]
    shape = jax.ShapeDtypeStruct
    first = lax.axis_index("gx") * leaves - leaves

    tangent = jnp.dot(
        positions.reshape(-1, P_SIZE), deriv_mat, precision=HIGHEST, preferred_element_type=F32
    ).reshape(3, count)
    jacobian = jnp.sqrt(1.0 + jnp.sum(tangent * tangent, axis=0))
    weighted = jnp.dot(
        forces.reshape(-1, P_SIZE), quad_mat, precision=HIGHEST, preferred_element_type=F32
    ).reshape(3, count)
    packed = jnp.concatenate(
        [positions.reshape(3, count), weighted * jacobian[None], jnp.zeros((2, count), F32)], axis=0
    )
    outgoing = pl.pallas_call(
        send_kernel,
        out_shape=shape((6 * slots // LANES, LANES), F32),
        in_specs=[SMEM, VMEM],
        out_specs=VMEM,
        scratch_shapes=[pltpu.VMEM((slots, LANES), F32), pltpu.VMEM((TILE, LANES), F32)],
        compiler_params=params(),
        name="send",
    )(point_dest.reshape(count), packed)
    arrived = exchange(outgoing, owners)

    source = tile_src.reshape(slots)
    centers = leaf_center.reshape(3 * leaves)
    sphere = RADIUS * sphere_points(SURF)
    surf_rows = jnp.pad(sphere, ((0, 5), (0, LANES - SURF)))
    surface = jnp.broadcast_to(surf_rows[:3, :SURF_PAD, None], (3, SURF_PAD, LANES))
    tiles, checks = pl.pallas_call(
        receive_kernel,
        out_shape=[shape((8 * leaves, LANES), F32), shape((3 * leaves, LANES), F32)],
        in_specs=[SMEM, SMEM, VMEM, VMEM, VMEM],
        out_specs=[VMEM, VMEM],
        scratch_shapes=[
            pltpu.VMEM((slots + 8, LANES), F32),
            pltpu.VMEM((2 * TILE, LANES), F32),
            pltpu.VMEM((64, LANES), F32),
        ],
        compiler_params=params(),
        name="receive",
    )(source, centers, arrived, surface, surf_rows)

    extended = halo(tiles, owners)
    check = checks.reshape(leaves, 3, LANES)[:, :, :SURF].reshape(leaves, expansion)
    multipole = jnp.dot(check, up_pinv, precision=HIGHEST, preferred_element_type=F32)
    multipole_ext = halo(multipole, owners)
    grouped = jnp.sum(multipole.reshape(leaves // 8, 8, expansion), axis=0)
    moment = jnp.einsum("ce,cef->f", grouped, child_ops, precision=HIGHEST)
    moment = jnp.pad(moment, (0, 8 * LANES - expansion)).reshape(8, LANES)
    coarse = lax.all_gather(moment, ("gx", "gy"), axis=0, tiled=True)

    near = near_sum(1, jnp.arange(leaves), tiles, tiles, [])
    places = (neighbours[0, 1:] - first).reshape(2 * leaves)
    near = near_sum(2, places, tiles, extended, [near])

    near, coarse, multipole_ext = lax.optimization_barrier((near, coarse, multipole_ext))
    coarse = coarse.reshape(-1, 8, LANES)[:, :2].reshape(-1, 2 * LANES)[:, :expansion]
    op_ids = jnp.arange(NOPS)
    onehot = (coarse_op[0, 0][:, None] == op_ids[None, :]).astype(F32)
    by_op = jnp.einsum("bk,be->ke", onehot, coarse, precision=HIGHEST)
    coarse_local = jnp.einsum("ke,kef->f", by_op, trans_ops, precision=HIGHEST)
    pushed = jnp.einsum("cfe,e->cf", child_ops, coarse_local, precision=HIGHEST)

    picked = jnp.take(multipole_ext, (inter_leaf[0] - first).T, axis=0)
    leaf_hot = (inter_op[0].T[:, :, None] == op_ids[None, None, :]).astype(F32)
    leaf_by_op = jnp.einsum("nje,njk->nke", picked, leaf_hot, precision=HIGHEST)
    local = jnp.dot(
        leaf_by_op.reshape(leaves, NOPS * expansion),
        trans_ops.reshape(NOPS * expansion, expansion),
        precision=HIGHEST,
        preferred_element_type=F32,
    )
    local = (local.reshape(leaves // 8, 8, expansion) + pushed[None]).reshape(leaves, 3, SURF)
    local = jnp.pad(local, ((0, 0), (0, 0), (0, LANES - SURF))).reshape(3 * leaves, LANES)

    returning = pl.pallas_call(
        far_kernel,
        out_shape=shape((3 * slots // LANES, LANES), F32),
        in_specs=[SMEM, SMEM, VMEM, VMEM, VMEM, VMEM, VMEM],
        out_specs=VMEM,
        scratch_shapes=[
            pltpu.VMEM((slots + 8, LANES), F32),
            pltpu.VMEM((2 * TILE, LANES), F32),
            pltpu.VMEM((80, LANES), F32),
        ],
        compiler_params=params(),
        name="far",
    )(source, centers, tiles, near, local, surface, surf_rows)
    came_back = exchange(returning, owners)
    velocity = pl.pallas_call(
        return_kernel,
        out_shape=shape((8, count), F32),
        in_specs=[SMEM, VMEM],
        out_specs=VMEM,
        scratch_shapes=[pltpu.VMEM((slots, LANES), F32), pltpu.VMEM((TILE, LANES), F32)],
        compiler_params=params(),
        name="back",
    )(point_dest.reshape(count), came_back)
    return velocity[:3].reshape(3, 1, count)


def solution(mesh):
    in_specs = (
        P(None, "gy", "gx"),
        P(None, "gy", "gx"),
        P(),
        P(),
        P("gy", "gx"),
        P(None, "gy", "gx"),
        P("gy", "gx"),
        P("gy", None, "gx"),
        P("gy", None, "gx"),
        P("gy", None, "gx"),
        P("gy", "gx", None),
        P(),
        P(),
        P(),
    )
    out_specs = P(None, "gy", "gx")
    return jax.shard_map(body, mesh=mesh, in_specs=in_specs, out_specs=out_specs, check_vma=False)
```

```python
import functools
import math

import jax
import jax.numpy as jnp
from jax import lax
from jax.experimental import pallas as pl
from jax.experimental.pallas import tpu as pltpu
from jax.sharding import PartitionSpec as P

P_SIZE = 544
NOPS = 16
TILE = 128
LANES = 128
SURF = 56
SURF_PAD = 64
GROUP = 4
SOFTENING = 0.25
RADIUS = 2.5
HIGHEST = lax.Precision.HIGHEST
F32 = jnp.float32
BF16 = jnp.bfloat16

VMEM = pl.BlockSpec(memory_space=pltpu.VMEM)
SMEM = pl.BlockSpec(memory_space=pltpu.SMEM)
ANY = pl.BlockSpec(memory_space=pl.ANY)


def params():
    return pltpu.CompilerParams(vmem_limit_bytes=60 * 1024 * 1024)


def sphere_points(count):
    index = jnp.arange(count).astype(F32)
    height = 1.0 - (2.0 * index + 1.0) / count
    radial = jnp.sqrt(1.0 - height * height)
    angle = 2.399963 * index
    return jnp.stack([radial * jnp.cos(angle), radial * jnp.sin(angle), height])


def aligned(index, step):
    return pl.multiple_of(index * step, step)


def split_bf16(value):
    high = value.astype(BF16)
    low = (value - high.astype(F32)).astype(BF16)
    return high, low


def dot_nt(left, right):
    return lax.dot_general(left, right, (((1,), (1,)), ((), ())), preferred_element_type=F32)


def dot_nn(left, right):
    return lax.dot_general(left, right, (((1,), (0,)), ((), ())), preferred_element_type=F32)


def move_rows(write, indices, block):
    for start in range(0, TILE, 8):
        part = indices.at[pl.ds(block * TILE + start, 8)]
        for row in range(8):
            write(start + row, part[row])


def to_rows_table(source, table, blocks, width):
    def one(block, carry):
        rows = source[pl.ds(block * width, width), :]
        table[pl.ds(aligned(block, TILE), TILE), 0:width] = rows.T
        return carry

    lax.fori_loop(0, blocks, one, 0, unroll=8)


def from_rows_table(table, out, blocks, width):
    def one(block, carry):
        rows = table[pl.ds(aligned(block, TILE), TILE), 0:8].T
        out[pl.ds(block * width, width), :] = rows[0:width]
        return carry

    lax.fori_loop(0, blocks, one, 0, unroll=8)


def send_kernel(dest, packed, out, table, stage):
    blocks = packed.shape[1] // LANES

    def one(block, carry):
        stage[:, 0:8] = packed[:, pl.ds(aligned(block, LANES), LANES)].T

        def write(row, index):
            table[pl.ds(index, 1), :] = stage[pl.ds(row, 1), :]

        move_rows(write, dest, block)
        return carry

    lax.fori_loop(0, blocks, one, 0)
    from_rows_table(table, out, out.shape[0] // 6, 6)


def features(x_rows, g_rows, store_a, store_d):
    gdotx = g_rows[0] * x_rows[0] + g_rows[1] * x_rows[1] + g_rows[2] * x_rows[2]
    for c in range(3):
        store_d(c, g_rows[c])
        store_a(c, gdotx * x_rows[c])
    for k in range(3):
        for c in range(3):
            store_a(3 + 3 * k + c, g_rows[k] * x_rows[c])
    for k in range(3):
        store_a(12 + k, g_rows[k])
    store_a(15, gdotx)


def combine(sums, y_rows):
    along = (
        y_rows[0] * sums[12:13] + y_rows[1] * sums[13:14] + y_rows[2] * sums[14:15] - sums[15:16]
    )
    flows = []
    for c in range(3):
        crossed = y_rows[0] * sums[3 + c : 4 + c]
        crossed = crossed + y_rows[1] * sums[6 + c : 7 + c]
        crossed = crossed + y_rows[2] * sums[9 + c : 10 + c]
        flows.append(sums[c : c + 1] + y_rows[c] * along - crossed)
    return flows


def pair_weights(dx, dy, dz):
    soft_sq = (dx * dx + dy * dy) + (dz * dz + SOFTENING)
    root = lax.rsqrt(soft_sq)
    cube = root * root * root
    return cube, root + SOFTENING * cube


def receive_kernel(source, centers, arrived, surface, surf_rows, tiles, checks, table, stage, feat):
    leaves = tiles.shape[0] // 8
    slots = leaves * TILE
    to_rows_table(arrived, table, slots // TILE, 6)
    table[pl.ds(slots, 8), :] = jnp.zeros((8, LANES), F32)
    feat[...] = jnp.zeros(feat.shape, F32)

    def gather(leaf, slot):
        def write(row, index):
            stage[pl.ds(slot * TILE + row, 1), :] = table[pl.ds(index, 1), :]

        move_rows(write, source, leaf)

    def check(leaf, slot):
        rows = stage[slot * TILE : slot * TILE + TILE, 0:8].T
        at = [rows[c : c + 1] for c in range(6)]
        size = at[0] * at[0] + at[1] * at[1] + at[2] * at[2] + 0.5 * SOFTENING
        along = at[0] * at[3] + at[1] * at[4] + at[2] * at[5]
        tiles[pl.ds(aligned(leaf, 8), 8), :] = jnp.concatenate([rows[0:6], size, -along])
        x_rows = [rows[c : c + 1] - centers[c * leaves + leaf] for c in range(3)]
        g_rows = [rows[3 + c : 4 + c] for c in range(3)]

        def store_a(row, value):
            feat[slot * 32 + row : slot * 32 + row + 1, :] = value

        def store_d(row, value):
            feat[slot * 32 + 16 + row : slot * 32 + 17 + row, :] = value

        features(x_rows, g_rows, store_a, store_d)
        both = feat[slot * 32 : slot * 32 + 32, :]
        high, low = split_bf16(both)
        cube, direct = pair_weights(
            surface[0] - x_rows[0], surface[1] - x_rows[1], surface[2] - x_rows[2]
        )
        cube_high, cube_low = split_bf16(cube)
        dir_high, dir_low = split_bf16(direct)
        sums = dot_nt(high[0:16], cube_high) + dot_nt(high[0:16], cube_low)
        sums = sums + dot_nt(low[0:16], cube_high) + dot_nt(high[16:32], dir_high)
        sums = sums + dot_nt(high[16:32], dir_low) + dot_nt(low[16:32], dir_high)
        flows = combine(sums, [surf_rows[c : c + 1, 0:SURF_PAD] for c in range(3)])
        for c in range(3):
            checks[pl.ds(leaf * 3 + c, 1), 0:SURF_PAD] = flows[c]

    def first_group(j, carry):
        gather(j, j)
        return carry

    lax.fori_loop(0, GROUP, first_group, 0)

    def two_groups(step, carry):
        leaf = step * 2 * GROUP
        for j in range(GROUP):
            gather(leaf + GROUP + j, GROUP + j)
        for j in range(GROUP):
            check(leaf + j, j)
        for j in range(GROUP):
            gather(jnp.minimum(leaf + 2 * GROUP + j, leaves - 1), j)
        for j in range(GROUP):
            check(leaf + GROUP + j, GROUP + j)
        return carry

    lax.fori_loop(0, leaves // (2 * GROUP), two_groups, 0)


def triple_split(value):
    first = value.astype(BF16).astype(F32)
    rest = value - first
    second = rest.astype(BF16).astype(F32)
    return first, second, (rest - second).astype(BF16).astype(F32)


def row_at(value, row):
    return jnp.broadcast_to(value[row : row + 1], (8, LANES))


def near_own_kernel(own, out):
    near_loop(1, None, own, own, None, out)


def near_others_kernel(places, previous, following, own, before, out, extended, sems):
    rows = own.shape[0]
    copies = [
        pltpu.make_async_copy(
            ref.at[pl.ds(0, rows), :], extended.at[pl.ds(n * rows, rows), :], sems.at[n]
        )
        for n, ref in enumerate((previous, own, following))
    ]
    for copy in copies:
        copy.start()
    for copy in copies:
        copy.wait()
    near_loop(2, places, own, extended, before, out)


def near_loop(listed, places, own, extended, before, out):
    leaves = own.shape[0] // 8
    row = lax.broadcasted_iota(jnp.int32, (8, LANES), 0)
    zero = jnp.zeros((8, LANES), F32)
    one_row = jnp.ones((8, LANES), F32)

    def one(leaf, carry):
        mine = own[pl.ds(aligned(leaf, 8), 8), :]
        parts = triple_split(mine)
        dist, push = [], []
        for part in parts:
            dist.append(jnp.where(row < 3, -2.0 * part, zero))
            turned = pltpu.roll(part, 3, 0)
            push.append(jnp.where((row >= 3) & (row < 6), turned, zero))
        dist_one = jnp.where(row == 6, 1.0, dist[0])
        push_one = jnp.where(row == 7, 1.0, push[0])
        squares = jnp.where(row == 0, row_at(parts[0], 6), zero)
        squares = jnp.where(row == 1, row_at(parts[1], 6), squares)
        squares = jnp.where(row == 2, row_at(parts[2], 6), squares)
        left = [dist_one] * 3 + [dist[1]] * 2 + [dist[2], squares, zero]
        right = [push_one] * 3 + [push[1]] * 2 + [push[2], zero, zero]
        targets = jnp.concatenate(
            [jnp.concatenate(left).astype(BF16), jnp.concatenate(right).astype(BF16)], axis=1
        )
        sums = jnp.zeros((16, 2 * LANES), F32)
        for n in range(listed):
            if places is None:
                high, mid, low = parts
            else:
                place = places[n * leaves + leaf]
                high, mid, low = triple_split(extended[pl.ds(aligned(place, 8), 8), :])
            sources = jnp.concatenate([high, mid, low, high, mid, high, one_row, zero]).astype(BF16)
            pairs = lax.dot_general(
                sources, targets, (((0,), (0,)), ((), ())), preferred_element_type=F32
            )
            root = lax.rsqrt(pairs[:, :LANES])
            cube = root * root * root
            direct = root + SOFTENING * cube
            both = jnp.concatenate([direct, cube * pairs[:, LANES:]], axis=1)
            both_high, both_low = split_bf16(both)
            weights = jnp.concatenate([jnp.where(row == 6, 1.0, high), jnp.where(row == 6, 0.0, mid)])
            weights = weights.astype(BF16)
            sums = sums + dot_nn(
                jnp.concatenate([weights, weights], axis=1),
                jnp.concatenate([both_high, both_low], axis=0),
            )
        total = sums[0:8] + sums[8:16]
        moved = total[:, LANES:]
        flow = pltpu.roll(total[:, :LANES], 5, 0) + (mine * row_at(moved, 6) - moved)
        if before is not None:
            flow = flow + before[pl.ds(aligned(leaf, 8), 8), :]
        out[pl.ds(aligned(leaf, 8), 8), :] = flow
        return carry

    lax.fori_loop(0, leaves, one, 0, unroll=8)


def far_kernel(source, centers, own, near, local, surface, surf_rows, out, table, stage, feat):
    leaves = own.shape[0] // 8
    scale = 1.0 / (8.0 * math.pi)
    feat[...] = jnp.zeros(feat.shape, F32)
    stage[...] = jnp.zeros(stage.shape, F32)

    def scatter(leaf, slot):
        def write(row, index):
            table[pl.ds(index, 1), :] = stage[pl.ds(slot * TILE + row, 1), :]

        move_rows(write, source, leaf)

    def far(leaf, slot):
        y_rows = [own[pl.ds(leaf * 8 + c, 1), :] - centers[c * leaves + leaf] for c in range(3)]
        g_rows = [local[pl.ds(leaf * 3 + c, 1), :] for c in range(3)]
        x_rows = [surf_rows[c : c + 1, :] for c in range(3)]

        def store_a(row, value):
            feat[slot * 32 + row : slot * 32 + row + 1, :] = value

        def store_d(row, value):
            feat[slot * 32 + 16 + row : slot * 32 + 17 + row, :] = value

        features(x_rows, g_rows, store_a, store_d)
        both = feat[slot * 32 : slot * 32 + 32, 0:SURF_PAD]
        high, low = split_bf16(both)
        cube, direct = pair_weights(
            y_rows[0] - surface[0], y_rows[1] - surface[1], y_rows[2] - surface[2]
        )
        cube_high, cube_low = split_bf16(cube)
        dir_high, dir_low = split_bf16(direct)
        sums = dot_nn(high[0:16], cube_high) + dot_nn(high[0:16], cube_low)
        sums = sums + dot_nn(low[0:16], cube_high) + dot_nn(high[16:32], dir_high)
        sums = sums + dot_nn(high[16:32], dir_low) + dot_nn(low[16:32], dir_high)
        flows = combine(sums, y_rows)
        total = [(flows[c] + near[pl.ds(leaf * 8 + c, 1), :]) * scale for c in range(3)]
        for c in range(3):
            feat[64 * GROUP + slot * 8 + c : 64 * GROUP + 1 + slot * 8 + c, :] = total[c]
        stage[slot * TILE : slot * TILE + TILE, 0:8] = feat[64 * GROUP + slot * 8 : 64 * GROUP + 8 + slot * 8, :].T

    for j in range(GROUP):
        far(j, j)

    def two_groups(step, carry):
        leaf = step * 2 * GROUP
        for j in range(GROUP):
            far(leaf + GROUP + j, GROUP + j)
        for j in range(GROUP):
            scatter(leaf + j, j)
        for j in range(GROUP):
            far(jnp.minimum(leaf + 2 * GROUP + j, leaves - 1), j)
        for j in range(GROUP):
            scatter(leaf + GROUP + j, GROUP + j)
        return carry

    lax.fori_loop(0, leaves // (2 * GROUP), two_groups, 0)
    from_rows_table(table, out, out.shape[0] // 3, 3)


def return_kernel(dest, arrived, out, table, stage):
    to_rows_table(arrived, table, arrived.shape[0] // 3, 3)

    def one(block, carry):
        def write(row, index):
            stage[pl.ds(row, 1), :] = table[pl.ds(index, 1), :]

        move_rows(write, dest, block)
        out[:, pl.ds(aligned(block, LANES), LANES)] = stage[:, 0:8].T
        return carry

    lax.fori_loop(0, out.shape[1] // LANES, one, 0)


def exchange(rows, owners):
    blocks = rows.reshape(owners, 1, -1)
    blocks = lax.all_to_all(blocks, "gx", split_axis=0, concat_axis=0, tiled=True)
    return blocks.reshape(rows.shape)


def near_own(tiles):
    return pl.pallas_call(
        near_own_kernel,
        out_shape=jax.ShapeDtypeStruct(tiles.shape, F32),
        in_specs=[VMEM],
        out_specs=VMEM,
        compiler_params=params(),
        cost_estimate=pl.CostEstimate(flops=10**10, transcendentals=0, bytes_accessed=10**7),
        name="near1",
    )(tiles)


def near_others(places, previous, following, tiles, before):
    return pl.pallas_call(
        near_others_kernel,
        out_shape=jax.ShapeDtypeStruct(tiles.shape, F32),
        in_specs=[SMEM, ANY, ANY, VMEM, VMEM],
        out_specs=VMEM,
        scratch_shapes=[
            pltpu.VMEM((3 * tiles.shape[0], LANES), F32),
            pltpu.SemaphoreType.DMA((3,)),
        ],
        compiler_params=params(),
        cost_estimate=pl.CostEstimate(flops=2 * 10**10, transcendentals=0, bytes_accessed=10**7),
        name="near2",
    )(places, previous, following, tiles, before)


def halo(shard, devices):
    up = [(i, i + 1) for i in range(devices - 1)]
    down = [(i + 1, i) for i in range(devices - 1)]
    return lax.ppermute(shard, "gx", up), lax.ppermute(shard, "gx", down)


def body(
    positions,
    forces,
    deriv_mat,
    quad_mat,
    point_dest,
    leaf_center,
    tile_src,
    neighbours,
    inter_leaf,
    inter_op,
    coarse_op,
    up_pinv,
    trans_ops,
    child_ops,
):
    owners = lax.axis_size("gx")
    count = positions.shape[2]
    leaves = leaf_center.shape[2]
    slots = leaves * TILE
    expansion = up_pinv.shape[0]
    shape = jax.ShapeDtypeStruct
    first = lax.axis_index("gx") * leaves - leaves

    tangent = jnp.dot(
        positions.reshape(-1, P_SIZE), deriv_mat, precision=HIGHEST, preferred_element_type=F32
    ).reshape(3, count)
    jacobian = jnp.sqrt(1.0 + jnp.sum(tangent * tangent, axis=0))
    weighted = jnp.dot(
        forces.reshape(-1, P_SIZE), quad_mat, precision=HIGHEST, preferred_element_type=F32
    ).reshape(3, count)
    packed = jnp.concatenate(
        [positions.reshape(3, count), weighted * jacobian[None], jnp.zeros((2, count), F32)], axis=0
    )
    outgoing = pl.pallas_call(
        send_kernel,
        out_shape=shape((6 * slots // LANES, LANES), F32),
        in_specs=[SMEM, VMEM],
        out_specs=VMEM,
        scratch_shapes=[pltpu.VMEM((slots, LANES), F32), pltpu.VMEM((TILE, LANES), F32)],
        compiler_params=params(),
        name="send",
    )(point_dest.reshape(count), packed)
    arrived = exchange(outgoing, owners)

    source = tile_src.reshape(slots)
    centers = leaf_center.reshape(3 * leaves)
    sphere = RADIUS * sphere_points(SURF)
    surf_rows = jnp.pad(sphere, ((0, 5), (0, LANES - SURF)))
    surface = jnp.broadcast_to(surf_rows[:3, :SURF_PAD, None], (3, SURF_PAD, LANES))
    tiles, checks = pl.pallas_call(
        receive_kernel,
        out_shape=[shape((8 * leaves, LANES), F32), shape((3 * leaves, LANES), F32)],
        in_specs=[SMEM, SMEM, VMEM, VMEM, VMEM],
        out_specs=[VMEM, VMEM],
        scratch_shapes=[
            pltpu.VMEM((slots + 8, LANES), F32),
            pltpu.VMEM((2 * GROUP * TILE, LANES), F32),
            pltpu.VMEM((2 * GROUP * 32, LANES), F32),
        ],
        compiler_params=params(),
        name="receive",
    )(source, centers, arrived, surface, surf_rows)

    check = checks.reshape(leaves, 3, LANES)[:, :, :SURF].reshape(leaves, expansion)
    multipole = jnp.dot(check, up_pinv, precision=HIGHEST, preferred_element_type=F32)
    halves = [multipole[:, :LANES], jnp.pad(multipole[:, LANES:], ((0, 0), (0, 2 * LANES - expansion)))]
    previous, following = halo(jnp.concatenate([tiles] + halves, axis=0), owners)
    grouped = jnp.sum(multipole.reshape(leaves // 8, 8, expansion), axis=0)
    moment = jnp.einsum("ce,cef->f", grouped, child_ops, precision=HIGHEST)
    moment = jnp.pad(moment, (0, 8 * LANES - expansion)).reshape(8, LANES)
    coarse = lax.all_gather(moment, ("gx", "gy"), axis=0, tiled=True)

    near = near_own(tiles)
    places = (neighbours[0, 1:] - first).reshape(2 * leaves)
    near = near_others(places, previous, following, tiles, near)
    near, coarse, previous, following = lax.optimization_barrier(
        (near, coarse, previous[8 * leaves :], following[8 * leaves :])
    )
    multipole_ext = jnp.concatenate(
        [
            jnp.concatenate([previous[:leaves], halves[0], following[:leaves]], axis=0),
            jnp.concatenate([previous[leaves:], halves[1], following[leaves:]], axis=0),
        ],
        axis=1,
    )
    coarse = coarse.reshape(-1, 8, LANES)[:, :2].reshape(-1, 2 * LANES)[:, :expansion]
    op_ids = jnp.arange(NOPS)
    onehot = (coarse_op[0, 0][:, None] == op_ids[None, :]).astype(F32)
    by_op = jnp.einsum("bk,be->ke", onehot, coarse, precision=HIGHEST)
    coarse_local = jnp.einsum("ke,kef->f", by_op, trans_ops, precision=HIGHEST)
    pushed = jnp.einsum("cfe,e->cf", child_ops, coarse_local, precision=HIGHEST)

    picked = jnp.take(multipole_ext, (inter_leaf[0] - first).T, axis=0)[:, :, :expansion]
    leaf_hot = (inter_op[0].T[:, :, None] == op_ids[None, None, :]).astype(F32)
    leaf_by_op = jnp.einsum("nje,njk->nke", picked, leaf_hot, precision=HIGHEST)
    local = jnp.dot(
        leaf_by_op.reshape(leaves, NOPS * expansion),
        trans_ops.reshape(NOPS * expansion, expansion),
        precision=HIGHEST,
        preferred_element_type=F32,
    )
    local = (local.reshape(leaves // 8, 8, expansion) + pushed[None]).reshape(leaves, 3, SURF)
    local = jnp.pad(local, ((0, 0), (0, 0), (0, LANES - SURF))).reshape(3 * leaves, LANES)

    returning = pl.pallas_call(
        far_kernel,
        out_shape=shape((3 * slots // LANES, LANES), F32),
        in_specs=[SMEM, SMEM, VMEM, VMEM, VMEM, VMEM, VMEM],
        out_specs=VMEM,
        scratch_shapes=[
            pltpu.VMEM((slots + 8, LANES), F32),
            pltpu.VMEM((2 * GROUP * TILE, LANES), F32),
            pltpu.VMEM((2 * GROUP * 40, LANES), F32),
        ],
        compiler_params=params(),
        name="far",
    )(source, centers, tiles, near, local, surface, surf_rows)
    came_back = exchange(returning, owners)
    velocity = pl.pallas_call(
        return_kernel,
        out_shape=shape((8, count), F32),
        in_specs=[SMEM, VMEM],
        out_specs=VMEM,
        scratch_shapes=[pltpu.VMEM((slots, LANES), F32), pltpu.VMEM((TILE, LANES), F32)],
        compiler_params=params(),
        name="back",
    )(point_dest.reshape(count), came_back)
    return velocity[:3].reshape(3, 1, count)


def solution(mesh):
    in_specs = (
        P(None, "gy", "gx"),
        P(None, "gy", "gx"),
        P(),
        P(),
        P("gy", "gx"),
        P(None, "gy", "gx"),
        P("gy", "gx"),
        P("gy", None, "gx"),
        P("gy", None, "gx"),
        P("gy", None, "gx"),
        P("gy", "gx", None),
        P(),
        P(),
        P(),
    )
    out_specs = P(None, "gy", "gx")
    return jax.shard_map(body, mesh=mesh, in_specs=in_specs, out_specs=out_specs, check_vma=False)
```

```python
import functools
import math

import jax
import jax.numpy as jnp
from jax import lax
from jax.experimental import pallas as pl
from jax.experimental.pallas import tpu as pltpu
from jax.sharding import PartitionSpec as P

P_SIZE = 544
NOPS = 16
TILE = 128
LANES = 128
SURF = 56
SURF_PAD = 64
GROUP = 8
SOFTENING = 0.25
RADIUS = 2.5
HIGHEST = lax.Precision.HIGHEST
F32 = jnp.float32
BF16 = jnp.bfloat16

VMEM = pl.BlockSpec(memory_space=pltpu.VMEM)
SMEM = pl.BlockSpec(memory_space=pltpu.SMEM)
ANY = pl.BlockSpec(memory_space=pl.ANY)


def params():
    return pltpu.CompilerParams(vmem_limit_bytes=60 * 1024 * 1024)


def sphere_points(count):
    index = jnp.arange(count).astype(F32)
    height = 1.0 - (2.0 * index + 1.0) / count
    radial = jnp.sqrt(1.0 - height * height)
    angle = 2.399963 * index
    return jnp.stack([radial * jnp.cos(angle), radial * jnp.sin(angle), height])


def aligned(index, step):
    return pl.multiple_of(index * step, step)


def split_bf16(value):
    high = value.astype(BF16)
    low = (value - high.astype(F32)).astype(BF16)
    return high, low


def dot_nt(left, right):
    return lax.dot_general(left, right, (((1,), (1,)), ((), ())), preferred_element_type=F32)


def dot_nn(left, right):
    return lax.dot_general(left, right, (((1,), (0,)), ((), ())), preferred_element_type=F32)


def move_rows(write, indices, block):
    for start in range(0, TILE, 8):
        part = indices.at[pl.ds(block * TILE + start, 8)]
        for row in range(8):
            write(start + row, part[row])


def pipelined(total, group, first, second, rolled):
    def start(j, carry):
        first(j, j)
        return carry

    if rolled:
        lax.fori_loop(0, group, start, 0)
    else:
        for j in range(group):
            first(j, j)

    def two_groups(step, carry):
        base = step * 2 * group
        for j in range(group):
            first(base + group + j, group + j)
        for j in range(group):
            second(base + j, j)
        for j in range(group):
            first(jnp.minimum(base + 2 * group + j, total - 1), j)
        for j in range(group):
            second(base + group + j, group + j)
        return carry

    lax.fori_loop(0, total // (2 * group), two_groups, 0)


def to_rows_table(source, table, blocks, width):
    def one(block, carry):
        rows = source[pl.ds(block * width, width), :]
        table[pl.ds(aligned(block, TILE), TILE), 0:width] = rows.T
        return carry

    lax.fori_loop(0, blocks, one, 0, unroll=8)


def from_rows_table(table, out, blocks, width):
    def one(block, carry):
        rows = table[pl.ds(aligned(block, TILE), TILE), 0:8].T
        out[pl.ds(block * width, width), :] = rows[0:width]
        return carry

    lax.fori_loop(0, blocks, one, 0, unroll=8)


def send_kernel(dest, packed, out, table, stage):
    blocks = packed.shape[1] // LANES

    def turn(block, slot):
        columns = packed[:, pl.ds(aligned(block, LANES), LANES)]
        stage[slot * TILE : slot * TILE + TILE, 0:8] = columns.T

    def scatter(block, slot):
        def write(row, index):
            table[pl.ds(index, 1), :] = stage[pl.ds(slot * TILE + row, 1), :]

        move_rows(write, dest, block)

    pipelined(blocks, 2, turn, scatter, False)
    from_rows_table(table, out, out.shape[0] // 6, 6)


def features(x_rows, g_rows, store_a, store_d):
    gdotx = g_rows[0] * x_rows[0] + g_rows[1] * x_rows[1] + g_rows[2] * x_rows[2]
    for c in range(3):
        store_d(c, g_rows[c])
        store_a(c, gdotx * x_rows[c])
    for k in range(3):
        for c in range(3):
            store_a(3 + 3 * k + c, g_rows[k] * x_rows[c])
    for k in range(3):
        store_a(12 + k, g_rows[k])
    store_a(15, gdotx)


def combine(sums, y_rows):
    along = (
        y_rows[0] * sums[12:13] + y_rows[1] * sums[13:14] + y_rows[2] * sums[14:15] - sums[15:16]
    )
    flows = []
    for c in range(3):
        crossed = y_rows[0] * sums[3 + c : 4 + c]
        crossed = crossed + y_rows[1] * sums[6 + c : 7 + c]
        crossed = crossed + y_rows[2] * sums[9 + c : 10 + c]
        flows.append(sums[c : c + 1] + y_rows[c] * along - crossed)
    return flows


def pair_weights(dx, dy, dz):
    soft_sq = (dx * dx + dy * dy) + (dz * dz + SOFTENING)
    root = lax.rsqrt(soft_sq)
    cube = root * root * root
    return cube, root + SOFTENING * cube


def receive_kernel(source, centers, arrived, surface, surf_rows, tiles, checks, table, stage, feat):
    leaves = tiles.shape[0] // 8
    slots = leaves * TILE
    to_rows_table(arrived, table, slots // TILE, 6)
    table[pl.ds(slots, 8), :] = jnp.zeros((8, LANES), F32)
    feat[...] = jnp.zeros(feat.shape, F32)

    def gather(leaf, slot):
        def write(row, index):
            stage[pl.ds(slot * TILE + row, 1), :] = table[pl.ds(index, 1), :]

        move_rows(write, source, leaf)

    def check(leaf, slot):
        rows = stage[slot * TILE : slot * TILE + TILE, 0:8].T
        at = [rows[c : c + 1] for c in range(6)]
        size = at[0] * at[0] + at[1] * at[1] + at[2] * at[2] + 0.5 * SOFTENING
        along = at[0] * at[3] + at[1] * at[4] + at[2] * at[5]
        tiles[pl.ds(aligned(leaf, 8), 8), :] = jnp.concatenate([rows[0:6], size, -along])
        x_rows = [rows[c : c + 1] - centers[c * leaves + leaf] for c in range(3)]
        g_rows = [rows[3 + c : 4 + c] for c in range(3)]

        def store_a(row, value):
            feat[slot * 32 + row : slot * 32 + row + 1, :] = value

        def store_d(row, value):
            feat[slot * 32 + 16 + row : slot * 32 + 17 + row, :] = value

        features(x_rows, g_rows, store_a, store_d)
        both = feat[slot * 32 : slot * 32 + 32, :]
        high, low = split_bf16(both)
        cube, direct = pair_weights(
            surface[0] - x_rows[0], surface[1] - x_rows[1], surface[2] - x_rows[2]
        )
        cube_high, cube_low = split_bf16(cube)
        dir_high, dir_low = split_bf16(direct)
        sums = dot_nt(high[0:16], cube_high) + dot_nt(high[0:16], cube_low)
        sums = sums + dot_nt(low[0:16], cube_high) + dot_nt(high[16:32], dir_high)
        sums = sums + dot_nt(high[16:32], dir_low) + dot_nt(low[16:32], dir_high)
        flows = combine(sums, [surf_rows[c : c + 1, 0:SURF_PAD] for c in range(3)])
        for c in range(3):
            checks[pl.ds(leaf * 3 + c, 1), 0:SURF_PAD] = flows[c]

    pipelined(leaves, GROUP, gather, check, True)


def triple_split(value):
    first = value.astype(BF16).astype(F32)
    rest = value - first
    second = rest.astype(BF16).astype(F32)
    return first, second, (rest - second).astype(BF16).astype(F32)


def row_at(value, row):
    return jnp.broadcast_to(value[row : row + 1], (8, LANES))


def near_own_kernel(own, out):
    near_loop(1, None, own, own, None, out)


def near_others_kernel(places, previous, following, own, before, out, extended, sems):
    rows = own.shape[0]
    copies = [
        pltpu.make_async_copy(
            ref.at[pl.ds(0, rows), :], extended.at[pl.ds(n * rows, rows), :], sems.at[n]
        )
        for n, ref in enumerate((previous, own, following))
    ]
    for copy in copies:
        copy.start()
    for copy in copies:
        copy.wait()
    near_loop(2, places, own, extended, before, out)


def near_loop(listed, places, own, extended, before, out):
    leaves = own.shape[0] // 8
    row = lax.broadcasted_iota(jnp.int32, (8, LANES), 0)
    zero = jnp.zeros((8, LANES), F32)
    one_row = jnp.ones((8, LANES), F32)

    def one(leaf, carry):
        mine = own[pl.ds(aligned(leaf, 8), 8), :]
        parts = triple_split(mine)
        dist, push = [], []
        for part in parts:
            dist.append(jnp.where(row < 3, -2.0 * part, zero))
            turned = pltpu.roll(part, 3, 0)
            push.append(jnp.where((row >= 3) & (row < 6), turned, zero))
        dist_one = jnp.where(row == 6, 1.0, dist[0])
        push_one = jnp.where(row == 7, 1.0, push[0])
        squares = jnp.where(row == 0, row_at(parts[0], 6), zero)
        squares = jnp.where(row == 1, row_at(parts[1], 6), squares)
        squares = jnp.where(row == 2, row_at(parts[2], 6), squares)
        left = [dist_one] * 3 + [dist[1]] * 2 + [dist[2], squares, zero]
        right = [push_one] * 3 + [push[1]] * 2 + [push[2], zero, zero]
        targets = jnp.concatenate(
            [jnp.concatenate(left).astype(BF16), jnp.concatenate(right).astype(BF16)], axis=1
        )
        sums = jnp.zeros((16, 2 * LANES), F32)
        for n in range(listed):
            if places is None:
                high, mid, low = parts
            else:
                place = places[n * leaves + leaf]
                high, mid, low = triple_split(extended[pl.ds(aligned(place, 8), 8), :])
            sources = jnp.concatenate([high, mid, low, high, mid, high, one_row, zero]).astype(BF16)
            pairs = lax.dot_general(
                sources, targets, (((0,), (0,)), ((), ())), preferred_element_type=F32
            )
            root = lax.rsqrt(pairs[:, :LANES])
            cube = root * root * root
            direct = root + SOFTENING * cube
            both = jnp.concatenate([direct, cube * pairs[:, LANES:]], axis=1)
            both_high, both_low = split_bf16(both)
            weights = jnp.concatenate([jnp.where(row == 6, 1.0, high), jnp.where(row == 6, 0.0, mid)])
            weights = weights.astype(BF16)
            sums = sums + dot_nn(
                jnp.concatenate([weights, weights], axis=1),
                jnp.concatenate([both_high, both_low], axis=0),
            )
        total = sums[0:8] + sums[8:16]
        moved = total[:, LANES:]
        flow = pltpu.roll(total[:, :LANES], 5, 0) + (mine * row_at(moved, 6) - moved)
        if before is not None:
            flow = flow + before[pl.ds(aligned(leaf, 8), 8), :]
        out[pl.ds(aligned(leaf, 8), 8), :] = flow
        return carry

    lax.fori_loop(0, leaves, one, 0, unroll=8)


def far_kernel(
    source, centers, own, near, local, pushed, surface, surf_rows, out, table, stage, feat
):
    leaves = own.shape[0] // 8
    scale = 1.0 / (8.0 * math.pi)
    feat[...] = jnp.zeros(feat.shape, F32)
    stage[...] = jnp.zeros(stage.shape, F32)

    def scatter(leaf, slot):
        def write(row, index):
            table[pl.ds(index, 1), :] = stage[pl.ds(slot * TILE + row, 1), :]

        move_rows(write, source, leaf)

    def far(leaf, slot):
        y_rows = [own[pl.ds(leaf * 8 + c, 1), :] - centers[c * leaves + leaf] for c in range(3)]
        child = slot % 8
        g_rows = [
            local[pl.ds(leaf * 3 + c, 1), :] + pushed[child * 3 + c : child * 3 + c + 1, :]
            for c in range(3)
        ]
        x_rows = [surf_rows[c : c + 1, :] for c in range(3)]

        def store_a(row, value):
            feat[slot * 32 + row : slot * 32 + row + 1, :] = value

        def store_d(row, value):
            feat[slot * 32 + 16 + row : slot * 32 + 17 + row, :] = value

        features(x_rows, g_rows, store_a, store_d)
        both = feat[slot * 32 : slot * 32 + 32, 0:SURF_PAD]
        high, low = split_bf16(both)
        cube, direct = pair_weights(
            y_rows[0] - surface[0], y_rows[1] - surface[1], y_rows[2] - surface[2]
        )
        cube_high, cube_low = split_bf16(cube)
        dir_high, dir_low = split_bf16(direct)
        sums = dot_nn(high[0:16], cube_high) + dot_nn(high[0:16], cube_low)
        sums = sums + dot_nn(low[0:16], cube_high) + dot_nn(high[16:32], dir_high)
        sums = sums + dot_nn(high[16:32], dir_low) + dot_nn(low[16:32], dir_high)
        flows = combine(sums, y_rows)
        total = [(flows[c] + near[pl.ds(leaf * 8 + c, 1), :]) * scale for c in range(3)]
        for c in range(3):
            feat[64 * GROUP + slot * 8 + c : 64 * GROUP + 1 + slot * 8 + c, :] = total[c]
        stage[slot * TILE : slot * TILE + TILE, 0:8] = feat[64 * GROUP + slot * 8 : 64 * GROUP + 8 + slot * 8, :].T

    pipelined(leaves, GROUP, far, scatter, False)
    from_rows_table(table, out, out.shape[0] // 3, 3)


def return_kernel(dest, arrived, out, table, stage):
    to_rows_table(arrived, table, arrived.shape[0] // 3, 3)
    blocks = out.shape[0] // 3

    def gather(block, slot):
        def write(row, index):
            stage[pl.ds(slot * TILE + row, 1), :] = table[pl.ds(index, 1), :]

        move_rows(write, dest, block)

    def turn(block, slot):
        rows = stage[slot * TILE : slot * TILE + TILE, 0:8].T
        for c in range(3):
            out[pl.ds(c * blocks + block, 1), :] = rows[c : c + 1]

    pipelined(blocks, 2, gather, turn, True)


def exchange(rows, owners):
    blocks = rows.reshape(owners, 1, -1)
    blocks = lax.all_to_all(blocks, "gx", split_axis=0, concat_axis=0, tiled=True)
    return blocks.reshape(rows.shape)


def near_own(tiles):
    return pl.pallas_call(
        near_own_kernel,
        out_shape=jax.ShapeDtypeStruct(tiles.shape, F32),
        in_specs=[VMEM],
        out_specs=VMEM,
        compiler_params=params(),
        cost_estimate=pl.CostEstimate(flops=10**10, transcendentals=0, bytes_accessed=10**7),
        name="near1",
    )(tiles)


def near_others(places, previous, following, tiles, before):
    return pl.pallas_call(
        near_others_kernel,
        out_shape=jax.ShapeDtypeStruct(tiles.shape, F32),
        in_specs=[SMEM, ANY, ANY, VMEM, VMEM],
        out_specs=VMEM,
        scratch_shapes=[
            pltpu.VMEM((3 * tiles.shape[0], LANES), F32),
            pltpu.SemaphoreType.DMA((3,)),
        ],
        compiler_params=params(),
        cost_estimate=pl.CostEstimate(flops=2 * 10**10, transcendentals=0, bytes_accessed=10**7),
        name="near2",
    )(places, previous, following, tiles, before)


def halo(shard, devices):
    up = [(i, i + 1) for i in range(devices - 1)]
    down = [(i + 1, i) for i in range(devices - 1)]
    return lax.ppermute(shard, "gx", up), lax.ppermute(shard, "gx", down)


def body(
    positions,
    forces,
    deriv_mat,
    quad_mat,
    point_dest,
    leaf_center,
    tile_src,
    neighbours,
    inter_leaf,
    inter_op,
    coarse_op,
    up_pinv,
    trans_ops,
    child_ops,
):
    owners = lax.axis_size("gx")
    count = positions.shape[2]
    leaves = leaf_center.shape[2]
    slots = leaves * TILE
    expansion = up_pinv.shape[0]
    shape = jax.ShapeDtypeStruct
    first = lax.axis_index("gx") * leaves - leaves

    tangent = jnp.dot(
        positions.reshape(-1, P_SIZE), deriv_mat, precision=HIGHEST, preferred_element_type=F32
    ).reshape(3, count)
    jacobian = jnp.sqrt(1.0 + jnp.sum(tangent * tangent, axis=0))
    weighted = jnp.dot(
        forces.reshape(-1, P_SIZE), quad_mat, precision=HIGHEST, preferred_element_type=F32
    ).reshape(3, count)
    packed = jnp.concatenate(
        [positions.reshape(3, count), weighted * jacobian[None], jnp.zeros((2, count), F32)], axis=0
    )
    outgoing = pl.pallas_call(
        send_kernel,
        out_shape=shape((6 * slots // LANES, LANES), F32),
        in_specs=[SMEM, VMEM],
        out_specs=VMEM,
        scratch_shapes=[pltpu.VMEM((slots, LANES), F32), pltpu.VMEM((4 * TILE, LANES), F32)],
        compiler_params=params(),
        name="send",
    )(point_dest.reshape(count), packed)
    arrived = exchange(outgoing, owners)

    source = tile_src.reshape(slots)
    centers = leaf_center.reshape(3 * leaves)
    sphere = RADIUS * sphere_points(SURF)
    surf_rows = jnp.pad(sphere, ((0, 5), (0, LANES - SURF)))
    surface = jnp.broadcast_to(surf_rows[:3, :SURF_PAD, None], (3, SURF_PAD, LANES))
    tiles, checks = pl.pallas_call(
        receive_kernel,
        out_shape=[shape((8 * leaves, LANES), F32), shape((3 * leaves, LANES), F32)],
        in_specs=[SMEM, SMEM, VMEM, VMEM, VMEM],
        out_specs=[VMEM, VMEM],
        scratch_shapes=[
            pltpu.VMEM((slots + 8, LANES), F32),
            pltpu.VMEM((2 * GROUP * TILE, LANES), F32),
            pltpu.VMEM((2 * GROUP * 32, LANES), F32),
        ],
        compiler_params=params(),
        name="receive",
    )(source, centers, arrived, surface, surf_rows)

    check = checks.reshape(leaves, 3, LANES)[:, :, :SURF].reshape(leaves, expansion)
    multipole = jnp.dot(check, up_pinv, precision=HIGHEST, preferred_element_type=F32)
    halves = [multipole[:, :LANES], jnp.pad(multipole[:, LANES:], ((0, 0), (0, 2 * LANES - expansion)))]
    grouped = jnp.sum(multipole.reshape(leaves // 8, 8, expansion), axis=0)
    moment = jnp.einsum("ce,cef->f", grouped, child_ops, precision=HIGHEST)
    moment = jnp.pad(moment, (0, 8 * LANES - expansion)).reshape(8, LANES)
    moment, *halves = lax.optimization_barrier((moment, *halves))
    coarse = lax.all_gather(moment, ("gx", "gy"), axis=0, tiled=True)
    previous, following = halo(jnp.concatenate([tiles] + halves, axis=0), owners)

    near = near_own(tiles)
    places = (neighbours[0, 1:] - first).reshape(2 * leaves)
    near = near_others(places, previous, following, tiles, near)
    sides = [previous[8 * leaves :], following[8 * leaves :]]
    multipole_ext = jnp.concatenate(
        [
            jnp.concatenate([sides[0][:leaves], halves[0], sides[1][:leaves]], axis=0),
            jnp.concatenate([sides[0][leaves:], halves[1], sides[1][leaves:]], axis=0),
        ],
        axis=1,
    )
    op_ids = jnp.arange(NOPS)
    picked = jnp.take(multipole_ext, (inter_leaf[0] - first).T, axis=0)[:, :, :expansion]
    leaf_hot = (inter_op[0].T[:, :, None] == op_ids[None, None, :]).astype(F32)
    leaf_by_op = jnp.einsum("nje,njk->nke", picked, leaf_hot, precision=HIGHEST)
    local = jnp.dot(
        leaf_by_op.reshape(leaves, NOPS * expansion),
        trans_ops.reshape(NOPS * expansion, expansion),
        precision=HIGHEST,
        preferred_element_type=F32,
    ).reshape(leaves, 3, SURF)
    local = jnp.pad(local, ((0, 0), (0, 0), (0, LANES - SURF))).reshape(3 * leaves, LANES)

    near, local, coarse = lax.optimization_barrier((near, local, coarse))
    coarse = coarse.reshape(-1, 8, LANES)[:, :2].reshape(-1, 2 * LANES)[:, :expansion]
    onehot = (coarse_op[0, 0][:, None] == op_ids[None, :]).astype(F32)
    by_op = jnp.einsum("bk,be->ke", onehot, coarse, precision=HIGHEST)
    coarse_local = jnp.einsum("ke,kef->f", by_op, trans_ops, precision=HIGHEST)
    pushed = jnp.einsum("cfe,e->cf", child_ops, coarse_local, precision=HIGHEST)
    pushed = jnp.pad(pushed.reshape(8, 3, SURF), ((0, 0), (0, 0), (0, LANES - SURF)))
    pushed = pushed.reshape(24, LANES)

    returning = pl.pallas_call(
        far_kernel,
        out_shape=shape((3 * slots // LANES, LANES), F32),
        in_specs=[SMEM, SMEM, VMEM, VMEM, VMEM, VMEM, VMEM, VMEM],
        out_specs=VMEM,
        scratch_shapes=[
            pltpu.VMEM((slots + 8, LANES), F32),
            pltpu.VMEM((2 * GROUP * TILE, LANES), F32),
            pltpu.VMEM((2 * GROUP * 40, LANES), F32),
        ],
        compiler_params=params(),
        name="far",
    )(source, centers, tiles, near, local, pushed, surface, surf_rows)
    came_back = exchange(returning, owners)
    velocity = pl.pallas_call(
        return_kernel,
        out_shape=shape((3 * count // LANES, LANES), F32),
        in_specs=[SMEM, VMEM],
        out_specs=VMEM,
        scratch_shapes=[pltpu.VMEM((slots, LANES), F32), pltpu.VMEM((4 * TILE, LANES), F32)],
        compiler_params=params(),
        name="back",
    )(point_dest.reshape(count), came_back)
    return velocity.reshape(3, 1, count)


def solution(mesh):
    in_specs = (
        P(None, "gy", "gx"),
        P(None, "gy", "gx"),
        P(),
        P(),
        P("gy", "gx"),
        P(None, "gy", "gx"),
        P("gy", "gx"),
        P("gy", None, "gx"),
        P("gy", None, "gx"),
        P("gy", None, "gx"),
        P("gy", "gx", None),
        P(),
        P(),
        P(),
    )
    out_specs = P(None, "gy", "gx")
    return jax.shard_map(body, mesh=mesh, in_specs=in_specs, out_specs=out_specs, check_vma=False)
```

```python
import functools
import math

import jax
import jax.numpy as jnp
from jax import lax
from jax.experimental import pallas as pl
from jax.experimental.pallas import tpu as pltpu
from jax.sharding import PartitionSpec as P

P_SIZE = 544
NOPS = 16
TILE = 128
LANES = 128
SURF = 56
SURF_PAD = 64
GROUP = 8
SOFTENING = 0.25
RADIUS = 2.5
HIGHEST = lax.Precision.HIGHEST
F32 = jnp.float32
BF16 = jnp.bfloat16

VMEM = pl.BlockSpec(memory_space=pltpu.VMEM)
SMEM = pl.BlockSpec(memory_space=pltpu.SMEM)
ANY = pl.BlockSpec(memory_space=pl.ANY)


def params():
    return pltpu.CompilerParams(vmem_limit_bytes=60 * 1024 * 1024)


def sphere_points(count):
    index = jnp.arange(count).astype(F32)
    height = 1.0 - (2.0 * index + 1.0) / count
    radial = jnp.sqrt(1.0 - height * height)
    angle = 2.399963 * index
    return jnp.stack([radial * jnp.cos(angle), radial * jnp.sin(angle), height])


def aligned(index, step):
    return pl.multiple_of(index * step, step)


def split_bf16(value):
    high = value.astype(BF16)
    low = (value - high.astype(F32)).astype(BF16)
    return high, low


def dot_nt(left, right):
    return lax.dot_general(left, right, (((1,), (1,)), ((), ())), preferred_element_type=F32)


def dot_nn(left, right):
    return lax.dot_general(left, right, (((1,), (0,)), ((), ())), preferred_element_type=F32)


def move_rows(write, indices, block):
    for start in range(0, TILE, 8):
        part = indices.at[pl.ds(block * TILE + start, 8)]
        for row in range(8):
            write(start + row, part[row])


def pipelined(total, group, first, second, rolled):
    def start(j, carry):
        first(j, j)
        return carry

    if rolled:
        lax.fori_loop(0, group, start, 0)
    else:
        for j in range(group):
            first(j, j)

    def two_groups(step, carry):
        base = step * 2 * group
        for j in range(group):
            first(base + group + j, group + j)
        for j in range(group):
            second(base + j, j)
        for j in range(group):
            first(jnp.minimum(base + 2 * group + j, total - 1), j)
        for j in range(group):
            second(base + group + j, group + j)
        return carry

    lax.fori_loop(0, total // (2 * group), two_groups, 0)


def to_rows_table(source, table, blocks, width):
    def one(block, carry):
        rows = source[pl.ds(block * width, width), :]
        table[pl.ds(aligned(block, TILE), TILE), 0:width] = rows.T
        return carry

    lax.fori_loop(0, blocks, one, 0, unroll=8)


def from_rows_table(table, out, blocks, width):
    def one(block, carry):
        rows = table[pl.ds(aligned(block, TILE), TILE), 0:8].T
        out[pl.ds(block * width, width), :] = rows[0:width]
        return carry

    lax.fori_loop(0, blocks, one, 0, unroll=8)


def send_kernel(dest, points, strengths, out, table, stage):
    blocks = points.shape[2] // LANES

    def turn(block, slot):
        lanes = pl.ds(aligned(block, LANES), LANES)
        columns = jnp.concatenate([points[c, :, lanes] for c in range(3)] + [strengths[:, lanes]])
        stage[slot * TILE : slot * TILE + TILE, 0:8] = columns.T

    def scatter(block, slot):
        def write(row, index):
            table[pl.ds(index, 1), :] = stage[pl.ds(slot * TILE + row, 1), :]

        move_rows(write, dest, block)

    pipelined(blocks, 2, turn, scatter, False)
    from_rows_table(table, out, out.shape[0] // 6, 6)


def features(x_rows, g_rows, store_a, store_d):
    gdotx = g_rows[0] * x_rows[0] + g_rows[1] * x_rows[1] + g_rows[2] * x_rows[2]
    for c in range(3):
        store_d(c, g_rows[c])
        store_a(c, gdotx * x_rows[c])
    for k in range(3):
        for c in range(3):
            store_a(3 + 3 * k + c, g_rows[k] * x_rows[c])
    for k in range(3):
        store_a(12 + k, g_rows[k])
    store_a(15, gdotx)


def combine(sums, y_rows):
    along = (
        y_rows[0] * sums[12:13] + y_rows[1] * sums[13:14] + y_rows[2] * sums[14:15] - sums[15:16]
    )
    flows = []
    for c in range(3):
        crossed = y_rows[0] * sums[3 + c : 4 + c]
        crossed = crossed + y_rows[1] * sums[6 + c : 7 + c]
        crossed = crossed + y_rows[2] * sums[9 + c : 10 + c]
        flows.append(sums[c : c + 1] + y_rows[c] * along - crossed)
    return flows


def pair_weights(dx, dy, dz):
    soft_sq = (dx * dx + dy * dy) + (dz * dz + SOFTENING)
    root = lax.rsqrt(soft_sq)
    cube = root * root * root
    return cube, root + SOFTENING * cube


def receive_kernel(source, centers, arrived, surface, surf_rows, tiles, checks, table, stage, feat):
    leaves = tiles.shape[0] // 8
    slots = leaves * TILE
    to_rows_table(arrived, table, slots // TILE, 6)
    table[pl.ds(slots, 8), :] = jnp.zeros((8, LANES), F32)
    feat[...] = jnp.zeros(feat.shape, F32)

    def gather(leaf, slot):
        def write(row, index):
            stage[pl.ds(slot * TILE + row, 1), :] = table[pl.ds(index, 1), :]

        move_rows(write, source, leaf)

    def check(leaf, slot):
        rows = stage[slot * TILE : slot * TILE + TILE, 0:8].T
        at = [rows[c : c + 1] for c in range(6)]
        size = at[0] * at[0] + at[1] * at[1] + at[2] * at[2] + 0.5 * SOFTENING
        along = at[0] * at[3] + at[1] * at[4] + at[2] * at[5]
        tiles[pl.ds(aligned(leaf, 8), 8), :] = jnp.concatenate([rows[0:6], size, -along])
        x_rows = [rows[c : c + 1] - centers[c * leaves + leaf] for c in range(3)]
        g_rows = [rows[3 + c : 4 + c] for c in range(3)]

        def store_a(row, value):
            feat[slot * 32 + row : slot * 32 + row + 1, :] = value

        def store_d(row, value):
            feat[slot * 32 + 16 + row : slot * 32 + 17 + row, :] = value

        features(x_rows, g_rows, store_a, store_d)
        both = feat[slot * 32 : slot * 32 + 32, :]
        high, low = split_bf16(both)
        cube, direct = pair_weights(
            surface[0] - x_rows[0], surface[1] - x_rows[1], surface[2] - x_rows[2]
        )
        cube_high, cube_low = split_bf16(cube)
        dir_high, dir_low = split_bf16(direct)
        sums = dot_nt(high[0:16], cube_high) + dot_nt(high[0:16], cube_low)
        sums = sums + dot_nt(low[0:16], cube_high) + dot_nt(high[16:32], dir_high)
        sums = sums + dot_nt(high[16:32], dir_low) + dot_nt(low[16:32], dir_high)
        flows = combine(sums, [surf_rows[c : c + 1, 0:SURF_PAD] for c in range(3)])
        for c in range(3):
            checks[pl.ds(leaf * 3 + c, 1), 0:SURF_PAD] = flows[c]

    pipelined(leaves, GROUP, gather, check, True)


def triple_split(value):
    first = value.astype(BF16).astype(F32)
    rest = value - first
    second = rest.astype(BF16).astype(F32)
    return first, second, (rest - second).astype(BF16).astype(F32)


def row_at(value, row):
    return jnp.broadcast_to(value[row : row + 1], (8, LANES))


def near_own_kernel(own, out):
    near_loop(1, None, own, own, None, out)


def near_others_kernel(places, previous, following, own, before, out, extended, sems):
    rows = own.shape[0]
    copies = [
        pltpu.make_async_copy(
            ref.at[pl.ds(0, rows), :], extended.at[pl.ds(n * rows, rows), :], sems.at[n]
        )
        for n, ref in enumerate((previous, own, following))
    ]
    for copy in copies:
        copy.start()
    for copy in copies:
        copy.wait()
    near_loop(2, places, own, extended, before, out)


def near_loop(listed, places, own, extended, before, out):
    leaves = own.shape[0] // 8
    row = lax.broadcasted_iota(jnp.int32, (8, LANES), 0)
    zero = jnp.zeros((8, LANES), F32)
    one_row = jnp.ones((8, LANES), F32)

    def one(leaf, carry):
        mine = own[pl.ds(aligned(leaf, 8), 8), :]
        parts = triple_split(mine)
        dist, push = [], []
        for part in parts:
            dist.append(jnp.where(row < 3, -2.0 * part, zero))
            turned = pltpu.roll(part, 3, 0)
            push.append(jnp.where((row >= 3) & (row < 6), turned, zero))
        dist_one = jnp.where(row == 6, 1.0, dist[0])
        push_one = jnp.where(row == 7, 1.0, push[0])
        squares = jnp.where(row == 0, row_at(parts[0], 6), zero)
        squares = jnp.where(row == 1, row_at(parts[1], 6), squares)
        squares = jnp.where(row == 2, row_at(parts[2], 6), squares)
        left = [dist_one] * 3 + [dist[1]] * 2 + [dist[2], squares, zero]
        right = [push_one] * 3 + [push[1]] * 2 + [push[2], zero, zero]
        targets = jnp.concatenate(
            [jnp.concatenate(left).astype(BF16), jnp.concatenate(right).astype(BF16)], axis=1
        )
        sums = jnp.zeros((16, 2 * LANES), F32)
        for n in range(listed):
            if places is None:
                high, mid, low = parts
            else:
                place = places[n * leaves + leaf]
                high, mid, low = triple_split(extended[pl.ds(aligned(place, 8), 8), :])
            sources = jnp.concatenate([high, mid, low, high, mid, high, one_row, zero]).astype(BF16)
            pairs = lax.dot_general(
                sources, targets, (((0,), (0,)), ((), ())), preferred_element_type=F32
            )
            root = lax.rsqrt(pairs[:, :LANES])
            cube = root * root * root
            direct = root + SOFTENING * cube
            both = jnp.concatenate([direct, cube * pairs[:, LANES:]], axis=1)
            both_high, both_low = split_bf16(both)
            weights = jnp.concatenate([jnp.where(row == 6, 1.0, high), jnp.where(row == 6, 0.0, mid)])
            weights = weights.astype(BF16)
            sums = sums + dot_nn(
                jnp.concatenate([weights, weights], axis=1),
                jnp.concatenate([both_high, both_low], axis=0),
            )
        total = sums[0:8] + sums[8:16]
        moved = total[:, LANES:]
        flow = pltpu.roll(total[:, :LANES], 5, 0) + (mine * row_at(moved, 6) - moved)
        if before is not None:
            flow = flow + before[pl.ds(aligned(leaf, 8), 8), :]
        out[pl.ds(aligned(leaf, 8), 8), :] = flow
        return carry

    lax.fori_loop(0, leaves, one, 0, unroll=8)


def far_kernel(
    source, centers, own, near, local, pushed, surface, surf_rows, out, table, stage, feat
):
    leaves = own.shape[0] // 8
    scale = 1.0 / (8.0 * math.pi)
    feat[...] = jnp.zeros(feat.shape, F32)
    stage[...] = jnp.zeros(stage.shape, F32)

    def scatter(leaf, slot):
        def write(row, index):
            table[pl.ds(index, 1), :] = stage[pl.ds(slot * TILE + row, 1), :]

        move_rows(write, source, leaf)

    def far(leaf, slot):
        y_rows = [own[pl.ds(leaf * 8 + c, 1), :] - centers[c * leaves + leaf] for c in range(3)]
        child = slot % 8
        g_rows = [
            local[pl.ds(leaf * 3 + c, 1), :] + pushed[child * 3 + c : child * 3 + c + 1, :]
            for c in range(3)
        ]
        x_rows = [surf_rows[c : c + 1, :] for c in range(3)]

        def store_a(row, value):
            feat[slot * 32 + row : slot * 32 + row + 1, :] = value

        def store_d(row, value):
            feat[slot * 32 + 16 + row : slot * 32 + 17 + row, :] = value

        features(x_rows, g_rows, store_a, store_d)
        both = feat[slot * 32 : slot * 32 + 32, 0:SURF_PAD]
        high, low = split_bf16(both)
        cube, direct = pair_weights(
            y_rows[0] - surface[0], y_rows[1] - surface[1], y_rows[2] - surface[2]
        )
        cube_high, cube_low = split_bf16(cube)
        dir_high, dir_low = split_bf16(direct)
        sums = dot_nn(high[0:16], cube_high) + dot_nn(high[0:16], cube_low)
        sums = sums + dot_nn(low[0:16], cube_high) + dot_nn(high[16:32], dir_high)
        sums = sums + dot_nn(high[16:32], dir_low) + dot_nn(low[16:32], dir_high)
        flows = combine(sums, y_rows)
        total = [(flows[c] + near[pl.ds(leaf * 8 + c, 1), :]) * scale for c in range(3)]
        for c in range(3):
            feat[64 * GROUP + slot * 8 + c : 64 * GROUP + 1 + slot * 8 + c, :] = total[c]
        stage[slot * TILE : slot * TILE + TILE, 0:8] = feat[64 * GROUP + slot * 8 : 64 * GROUP + 8 + slot * 8, :].T

    pipelined(leaves, GROUP, far, scatter, False)
    from_rows_table(table, out, out.shape[0] // 3, 3)


def return_kernel(dest, arrived, out, table, stage):
    to_rows_table(arrived, table, arrived.shape[0] // 3, 3)
    blocks = out.shape[2] // LANES

    def gather(block, slot):
        def write(row, index):
            stage[pl.ds(slot * TILE + row, 1), :] = table[pl.ds(index, 1), :]

        move_rows(write, dest, block)

    def turn(block, slot):
        rows = stage[slot * TILE : slot * TILE + TILE, 0:8].T
        for c in range(3):
            out[c, :, pl.ds(aligned(block, LANES), LANES)] = rows[c : c + 1]

    pipelined(blocks, 2, gather, turn, True)


def exchange(rows, owners):
    blocks = rows.reshape(owners, 1, -1)
    blocks = lax.all_to_all(blocks, "gx", split_axis=0, concat_axis=0, tiled=True)
    return blocks.reshape(rows.shape)


def near_own(tiles):
    return pl.pallas_call(
        near_own_kernel,
        out_shape=jax.ShapeDtypeStruct(tiles.shape, F32),
        in_specs=[VMEM],
        out_specs=VMEM,
        compiler_params=params(),
        cost_estimate=pl.CostEstimate(flops=10**10, transcendentals=0, bytes_accessed=10**7),
        name="near1",
    )(tiles)


def near_others(places, previous, following, tiles, before):
    return pl.pallas_call(
        near_others_kernel,
        out_shape=jax.ShapeDtypeStruct(tiles.shape, F32),
        in_specs=[SMEM, ANY, ANY, VMEM, VMEM],
        out_specs=VMEM,
        scratch_shapes=[
            pltpu.VMEM((3 * tiles.shape[0], LANES), F32),
            pltpu.SemaphoreType.DMA((3,)),
        ],
        compiler_params=params(),
        cost_estimate=pl.CostEstimate(flops=2 * 10**10, transcendentals=0, bytes_accessed=10**7),
        name="near2",
    )(places, previous, following, tiles, before)


def halo(shard, devices):
    up = [(i, i + 1) for i in range(devices - 1)]
    down = [(i + 1, i) for i in range(devices - 1)]
    return lax.ppermute(shard, "gx", up), lax.ppermute(shard, "gx", down)


def body(
    positions,
    forces,
    deriv_mat,
    quad_mat,
    point_dest,
    leaf_center,
    tile_src,
    neighbours,
    inter_leaf,
    inter_op,
    coarse_op,
    up_pinv,
    trans_ops,
    child_ops,
):
    owners = lax.axis_size("gx")
    count = positions.shape[2]
    leaves = leaf_center.shape[2]
    slots = leaves * TILE
    expansion = up_pinv.shape[0]
    shape = jax.ShapeDtypeStruct
    first = lax.axis_index("gx") * leaves - leaves

    tangent = jnp.dot(
        positions.reshape(-1, P_SIZE), deriv_mat, precision=HIGHEST, preferred_element_type=F32
    ).reshape(3, count)
    jacobian = jnp.sqrt(1.0 + jnp.sum(tangent * tangent, axis=0))
    weighted = jnp.dot(
        forces.reshape(-1, P_SIZE), quad_mat, precision=HIGHEST, preferred_element_type=F32
    ).reshape(3, count)
    strengths = jnp.pad(weighted * jacobian[None], ((0, 2), (0, 0)))
    outgoing = pl.pallas_call(
        send_kernel,
        out_shape=shape((6 * slots // LANES, LANES), F32),
        in_specs=[SMEM, VMEM, VMEM],
        out_specs=VMEM,
        scratch_shapes=[pltpu.VMEM((slots, LANES), F32), pltpu.VMEM((4 * TILE, LANES), F32)],
        compiler_params=params(),
        name="send",
    )(point_dest.reshape(count), positions, strengths)
    arrived = exchange(outgoing, owners)

    source = tile_src.reshape(slots)
    centers = leaf_center.reshape(3 * leaves)
    sphere = RADIUS * sphere_points(SURF)
    surf_rows = jnp.pad(sphere, ((0, 5), (0, LANES - SURF)))
    surface = jnp.broadcast_to(surf_rows[:3, :SURF_PAD, None], (3, SURF_PAD, LANES))
    tiles, checks = pl.pallas_call(
        receive_kernel,
        out_shape=[shape((8 * leaves, LANES), F32), shape((3 * leaves, LANES), F32)],
        in_specs=[SMEM, SMEM, VMEM, VMEM, VMEM],
        out_specs=[VMEM, VMEM],
        scratch_shapes=[
            pltpu.VMEM((slots + 8, LANES), F32),
            pltpu.VMEM((2 * GROUP * TILE, LANES), F32),
            pltpu.VMEM((2 * GROUP * 32, LANES), F32),
        ],
        compiler_params=params(),
        name="receive",
    )(source, centers, arrived, surface, surf_rows)

    check = checks.reshape(leaves, 3, LANES)[:, :, :SURF].reshape(leaves, expansion)
    multipole = jnp.dot(check, up_pinv, precision=HIGHEST, preferred_element_type=F32)
    halves = [multipole[:, :LANES], jnp.pad(multipole[:, LANES:], ((0, 0), (0, 2 * LANES - expansion)))]
    grouped = jnp.sum(multipole.reshape(leaves // 8, 8, expansion), axis=0)
    moment = jnp.einsum("ce,cef->f", grouped, child_ops, precision=HIGHEST)
    moment = jnp.pad(moment, (0, 8 * LANES - expansion)).reshape(8, LANES)
    moment, *halves = lax.optimization_barrier((moment, *halves))
    coarse = lax.all_gather(moment, ("gx", "gy"), axis=0, tiled=True)
    previous, following = halo(jnp.concatenate([tiles] + halves, axis=0), owners)

    near = near_own(tiles)
    places = (neighbours[0, 1:] - first).reshape(2 * leaves)
    near = near_others(places, previous, following, tiles, near)
    sides = [previous[8 * leaves :], following[8 * leaves :]]
    multipole_ext = jnp.concatenate(
        [
            jnp.concatenate([sides[0][:leaves], halves[0], sides[1][:leaves]], axis=0),
            jnp.concatenate([sides[0][leaves:], halves[1], sides[1][leaves:]], axis=0),
        ],
        axis=1,
    )
    op_ids = jnp.arange(NOPS)
    picked = jnp.take(multipole_ext, (inter_leaf[0] - first).T, axis=0)[:, :, :expansion]
    leaf_hot = (inter_op[0].T[:, :, None] == op_ids[None, None, :]).astype(F32)
    leaf_by_op = jnp.einsum("nje,njk->nke", picked, leaf_hot, precision=HIGHEST)
    local = jnp.dot(
        leaf_by_op.reshape(leaves, NOPS * expansion),
        trans_ops.reshape(NOPS * expansion, expansion),
        precision=HIGHEST,
        preferred_element_type=F32,
    ).reshape(leaves, 3, SURF)
    local = jnp.pad(local, ((0, 0), (0, 0), (0, LANES - SURF))).reshape(3 * leaves, LANES)

    near, local, coarse = lax.optimization_barrier((near, local, coarse))
    coarse = coarse.reshape(-1, 8, LANES)[:, :2].reshape(-1, 2 * LANES)[:, :expansion]
    onehot = (coarse_op[0, 0][:, None] == op_ids[None, :]).astype(F32)
    by_op = jnp.einsum("bk,be->ke", onehot, coarse, precision=HIGHEST)
    coarse_local = jnp.einsum("ke,kef->f", by_op, trans_ops, precision=HIGHEST)
    pushed = jnp.einsum("cfe,e->cf", child_ops, coarse_local, precision=HIGHEST)
    pushed = jnp.pad(pushed.reshape(8, 3, SURF), ((0, 0), (0, 0), (0, LANES - SURF)))
    pushed = pushed.reshape(24, LANES)

    returning = pl.pallas_call(
        far_kernel,
        out_shape=shape((3 * slots // LANES, LANES), F32),
        in_specs=[SMEM, SMEM, VMEM, VMEM, VMEM, VMEM, VMEM, VMEM],
        out_specs=VMEM,
        scratch_shapes=[
            pltpu.VMEM((slots + 8, LANES), F32),
            pltpu.VMEM((2 * GROUP * TILE, LANES), F32),
            pltpu.VMEM((2 * GROUP * 40, LANES), F32),
        ],
        compiler_params=params(),
        name="far",
    )(source, centers, tiles, near, local, pushed, surface, surf_rows)
    came_back = exchange(returning, owners)
    velocity = pl.pallas_call(
        return_kernel,
        out_shape=shape((3, 1, count), F32),
        in_specs=[SMEM, VMEM],
        out_specs=VMEM,
        scratch_shapes=[pltpu.VMEM((slots, LANES), F32), pltpu.VMEM((4 * TILE, LANES), F32)],
        compiler_params=params(),
        name="back",
    )(point_dest.reshape(count), came_back)
    return velocity


def solution(mesh):
    in_specs = (
        P(None, "gy", "gx"),
        P(None, "gy", "gx"),
        P(),
        P(),
        P("gy", "gx"),
        P(None, "gy", "gx"),
        P("gy", "gx"),
        P("gy", None, "gx"),
        P("gy", None, "gx"),
        P("gy", None, "gx"),
        P("gy", "gx", None),
        P(),
        P(),
        P(),
    )
    out_specs = P(None, "gy", "gx")
    return jax.shard_map(body, mesh=mesh, in_specs=in_specs, out_specs=out_specs, check_vma=False)
```

```python
import functools
import math

import jax
import jax.numpy as jnp
from jax import lax
from jax.experimental import pallas as pl
from jax.experimental.pallas import tpu as pltpu
from jax.sharding import PartitionSpec as P

P_SIZE = 544
NOPS = 16
TILE = 128
LANES = 128
SURF = 56
SURF_PAD = 64
GROUP = 8
RECEIVE_GROUP = 16
SOFTENING = 0.25
RADIUS = 2.5
HIGHEST = lax.Precision.HIGHEST
F32 = jnp.float32
BF16 = jnp.bfloat16

VMEM = pl.BlockSpec(memory_space=pltpu.VMEM)
SMEM = pl.BlockSpec(memory_space=pltpu.SMEM)
ANY = pl.BlockSpec(memory_space=pl.ANY)


def params():
    return pltpu.CompilerParams(vmem_limit_bytes=60 * 1024 * 1024)


def sphere_points(count):
    index = jnp.arange(count).astype(F32)
    height = 1.0 - (2.0 * index + 1.0) / count
    radial = jnp.sqrt(1.0 - height * height)
    angle = 2.399963 * index
    return jnp.stack([radial * jnp.cos(angle), radial * jnp.sin(angle), height])


def aligned(index, step):
    return pl.multiple_of(index * step, step)


def split_bf16(value):
    high = value.astype(BF16)
    low = (value - high.astype(F32)).astype(BF16)
    return high, low


def dot_nt(left, right):
    return lax.dot_general(left, right, (((1,), (1,)), ((), ())), preferred_element_type=F32)


def dot_nn(left, right):
    return lax.dot_general(left, right, (((1,), (0,)), ((), ())), preferred_element_type=F32)


def move_rows(write, indices, block):
    for start in range(0, TILE, 8):
        part = indices.at[pl.ds(block * TILE + start, 8)]
        for row in range(8):
            write(start + row, part[row])


def pipelined(total, group, first, second, rolled):
    def start(j, carry):
        first(j, j)
        return carry

    if rolled:
        lax.fori_loop(0, group, start, 0)
    else:
        for j in range(group):
            first(j, j)

    def two_groups(step, carry):
        base = step * 2 * group
        for j in range(group):
            first(base + group + j, group + j)
        for j in range(group):
            second(base + j, j)
        for j in range(group):
            first(jnp.minimum(base + 2 * group + j, total - 1), j)
        for j in range(group):
            second(base + group + j, group + j)
        return carry

    lax.fori_loop(0, total // (2 * group), two_groups, 0)


def to_rows_table(source, table, blocks, width):
    def one(block, carry):
        rows = source[pl.ds(block * width, width), :]
        table[pl.ds(aligned(block, TILE), TILE), 0:width] = rows.T
        return carry

    lax.fori_loop(0, blocks, one, 0, unroll=8)


def from_rows_table(table, out, blocks, width):
    def one(block, carry):
        rows = table[pl.ds(aligned(block, TILE), TILE), 0:8].T
        out[pl.ds(block * width, width), :] = rows[0:width]
        return carry

    lax.fori_loop(0, blocks, one, 0, unroll=8)


def send_kernel(dest, points, strengths, out, table, stage):
    blocks = points.shape[2] // LANES

    def turn(block, slot):
        lanes = pl.ds(aligned(block, LANES), LANES)
        columns = jnp.concatenate([points[c, :, lanes] for c in range(3)] + [strengths[:, lanes]])
        stage[slot * TILE : slot * TILE + TILE, 0:8] = columns.T

    def scatter(block, slot):
        def write(row, index):
            table[pl.ds(index, 1), :] = stage[pl.ds(slot * TILE + row, 1), :]

        move_rows(write, dest, block)

    pipelined(blocks, 2, turn, scatter, False)
    from_rows_table(table, out, out.shape[0] // 6, 6)


def features(x_rows, g_rows, store_a, store_d):
    gdotx = g_rows[0] * x_rows[0] + g_rows[1] * x_rows[1] + g_rows[2] * x_rows[2]
    for c in range(3):
        store_d(c, g_rows[c])
        store_a(c, gdotx * x_rows[c])
    for k in range(3):
        for c in range(3):
            store_a(3 + 3 * k + c, g_rows[k] * x_rows[c])
    for k in range(3):
        store_a(12 + k, g_rows[k])
    store_a(15, gdotx)


def combine(sums, y_rows):
    along = (
        y_rows[0] * sums[12:13] + y_rows[1] * sums[13:14] + y_rows[2] * sums[14:15] - sums[15:16]
    )
    flows = []
    for c in range(3):
        crossed = y_rows[0] * sums[3 + c : 4 + c]
        crossed = crossed + y_rows[1] * sums[6 + c : 7 + c]
        crossed = crossed + y_rows[2] * sums[9 + c : 10 + c]
        flows.append(sums[c : c + 1] + y_rows[c] * along - crossed)
    return flows


def pair_weights(dx, dy, dz):
    soft_sq = (dx * dx + dy * dy) + (dz * dz + SOFTENING)
    root = lax.rsqrt(soft_sq)
    cube = root * root * root
    return cube, root + SOFTENING * cube


def receive_kernel(source, centers, arrived, surface, surf_rows, tiles, checks, table, stage, feat):
    leaves = tiles.shape[0] // 8
    slots = leaves * TILE
    to_rows_table(arrived, table, slots // TILE, 6)
    table[pl.ds(slots, 8), :] = jnp.zeros((8, LANES), F32)
    feat[...] = jnp.zeros(feat.shape, F32)

    def gather(leaf, slot):
        def write(row, index):
            stage[pl.ds(slot * TILE + row, 1), :] = table[pl.ds(index, 1), :]

        move_rows(write, source, leaf)

    def check(leaf, slot):
        rows = stage[slot * TILE : slot * TILE + TILE, 0:8].T
        at = [rows[c : c + 1] for c in range(6)]
        size = at[0] * at[0] + at[1] * at[1] + at[2] * at[2] + 0.5 * SOFTENING
        along = at[0] * at[3] + at[1] * at[4] + at[2] * at[5]
        tiles[pl.ds(aligned(leaf, 8), 8), :] = jnp.concatenate([rows[0:6], size, -along])
        x_rows = [rows[c : c + 1] - centers[c * leaves + leaf] for c in range(3)]
        g_rows = [rows[3 + c : 4 + c] for c in range(3)]

        def store_a(row, value):
            feat[slot * 32 + row : slot * 32 + row + 1, :] = value

        def store_d(row, value):
            feat[slot * 32 + 16 + row : slot * 32 + 17 + row, :] = value

        features(x_rows, g_rows, store_a, store_d)
        both = feat[slot * 32 : slot * 32 + 32, :]
        high, low = split_bf16(both)
        cube, direct = pair_weights(
            surface[0] - x_rows[0], surface[1] - x_rows[1], surface[2] - x_rows[2]
        )
        cube_high, cube_low = split_bf16(cube)
        dir_high, dir_low = split_bf16(direct)
        sums = dot_nt(high[0:16], cube_high) + dot_nt(high[0:16], cube_low)
        sums = sums + dot_nt(low[0:16], cube_high) + dot_nt(high[16:32], dir_high)
        sums = sums + dot_nt(high[16:32], dir_low) + dot_nt(low[16:32], dir_high)
        flows = combine(sums, [surf_rows[c : c + 1, 0:SURF_PAD] for c in range(3)])
        for c in range(3):
            checks[pl.ds(leaf * 3 + c, 1), 0:SURF_PAD] = flows[c]

    pipelined(leaves, RECEIVE_GROUP, gather, check, True)


def triple_split(value):
    first = value.astype(BF16).astype(F32)
    rest = value - first
    second = rest.astype(BF16).astype(F32)
    return first, second, (rest - second).astype(BF16).astype(F32)


def row_at(value, row):
    return jnp.broadcast_to(value[row : row + 1], (8, LANES))


def near_own_kernel(own, out):
    near_loop(1, None, own, own, None, out)


def near_others_kernel(places, previous, following, own, before, out, extended, sems):
    rows = own.shape[0]
    copies = [
        pltpu.make_async_copy(
            ref.at[pl.ds(0, rows), :], extended.at[pl.ds(n * rows, rows), :], sems.at[n]
        )
        for n, ref in enumerate((previous, own, following))
    ]
    for copy in copies:
        copy.start()
    for copy in copies:
        copy.wait()
    near_loop(2, places, own, extended, before, out)


def near_loop(listed, places, own, extended, before, out):
    leaves = own.shape[0] // 8
    row = lax.broadcasted_iota(jnp.int32, (8, LANES), 0)
    zero = jnp.zeros((8, LANES), F32)
    one_row = jnp.ones((8, LANES), F32)

    def one(leaf, carry):
        mine = own[pl.ds(aligned(leaf, 8), 8), :]
        parts = triple_split(mine)
        dist, push = [], []
        for part in parts:
            dist.append(jnp.where(row < 3, -2.0 * part, zero))
            turned = pltpu.roll(part, 3, 0)
            push.append(jnp.where((row >= 3) & (row < 6), turned, zero))
        dist_one = jnp.where(row == 6, 1.0, dist[0])
        push_one = jnp.where(row == 7, 1.0, push[0])
        squares = jnp.where(row == 0, row_at(parts[0], 6), zero)
        squares = jnp.where(row == 1, row_at(parts[1], 6), squares)
        squares = jnp.where(row == 2, row_at(parts[2], 6), squares)
        left = [dist_one] * 3 + [dist[1]] * 2 + [dist[2], squares, zero]
        right = [push_one] * 3 + [push[1]] * 2 + [push[2], zero, zero]
        targets = jnp.concatenate(
            [jnp.concatenate(left).astype(BF16), jnp.concatenate(right).astype(BF16)], axis=1
        )
        sums = jnp.zeros((16, 2 * LANES), F32)
        for n in range(listed):
            if places is None:
                high, mid, low = parts
            else:
                place = places[n * leaves + leaf]
                high, mid, low = triple_split(extended[pl.ds(aligned(place, 8), 8), :])
            sources = jnp.concatenate([high, mid, low, high, mid, high, one_row, zero]).astype(BF16)
            pairs = lax.dot_general(
                sources, targets, (((0,), (0,)), ((), ())), preferred_element_type=F32
            )
            root = lax.rsqrt(pairs[:, :LANES])
            cube = root * root * root
            direct = root + SOFTENING * cube
            both = jnp.concatenate([direct, cube * pairs[:, LANES:]], axis=1)
            both_high, both_low = split_bf16(both)
            weights = jnp.concatenate([jnp.where(row == 6, 1.0, high), jnp.where(row == 6, 0.0, mid)])
            weights = weights.astype(BF16)
            sums = sums + dot_nn(
                jnp.concatenate([weights, weights], axis=1),
                jnp.concatenate([both_high, both_low], axis=0),
            )
        total = sums[0:8] + sums[8:16]
        moved = total[:, LANES:]
        flow = pltpu.roll(total[:, :LANES], 5, 0) + (mine * row_at(moved, 6) - moved)
        if before is not None:
            flow = flow + before[pl.ds(aligned(leaf, 8), 8), :]
        out[pl.ds(aligned(leaf, 8), 8), :] = flow
        return carry

    lax.fori_loop(0, leaves, one, 0, unroll=8)


def far_kernel(
    source, centers, own, near, local, pushed, surface, surf_rows, out, table, stage, feat
):
    leaves = own.shape[0] // 8
    scale = 1.0 / (8.0 * math.pi)
    feat[...] = jnp.zeros(feat.shape, F32)
    stage[...] = jnp.zeros(stage.shape, F32)

    def scatter(leaf, slot):
        def write(row, index):
            table[pl.ds(index, 1), :] = stage[pl.ds(slot * TILE + row, 1), :]

        move_rows(write, source, leaf)

    def far(leaf, slot):
        y_rows = [own[pl.ds(leaf * 8 + c, 1), :] - centers[c * leaves + leaf] for c in range(3)]
        child = slot % 8
        g_rows = [
            local[pl.ds(leaf * 3 + c, 1), :] + pushed[child * 3 + c : child * 3 + c + 1, :]
            for c in range(3)
        ]
        x_rows = [surf_rows[c : c + 1, :] for c in range(3)]

        def store_a(row, value):
            feat[slot * 32 + row : slot * 32 + row + 1, :] = value

        def store_d(row, value):
            feat[slot * 32 + 16 + row : slot * 32 + 17 + row, :] = value

        features(x_rows, g_rows, store_a, store_d)
        both = feat[slot * 32 : slot * 32 + 32, 0:SURF_PAD]
        high, low = split_bf16(both)
        cube, direct = pair_weights(
            y_rows[0] - surface[0], y_rows[1] - surface[1], y_rows[2] - surface[2]
        )
        cube_high, cube_low = split_bf16(cube)
        dir_high, dir_low = split_bf16(direct)
        sums = dot_nn(high[0:16], cube_high) + dot_nn(high[0:16], cube_low)
        sums = sums + dot_nn(low[0:16], cube_high) + dot_nn(high[16:32], dir_high)
        sums = sums + dot_nn(high[16:32], dir_low) + dot_nn(low[16:32], dir_high)
        flows = combine(sums, y_rows)
        total = [(flows[c] + near[pl.ds(leaf * 8 + c, 1), :]) * scale for c in range(3)]
        for c in range(3):
            feat[64 * GROUP + slot * 8 + c : 64 * GROUP + 1 + slot * 8 + c, :] = total[c]
        stage[slot * TILE : slot * TILE + TILE, 0:8] = feat[64 * GROUP + slot * 8 : 64 * GROUP + 8 + slot * 8, :].T

    pipelined(leaves, GROUP, far, scatter, False)
    from_rows_table(table, out, out.shape[0] // 3, 3)


def return_kernel(dest, arrived, out, table, stage):
    to_rows_table(arrived, table, arrived.shape[0] // 3, 3)
    blocks = out.shape[2] // LANES

    def gather(block, slot):
        def write(row, index):
            stage[pl.ds(slot * TILE + row, 1), :] = table[pl.ds(index, 1), :]

        move_rows(write, dest, block)

    def turn(block, slot):
        rows = stage[slot * TILE : slot * TILE + TILE, 0:8].T
        for c in range(3):
            out[c, :, pl.ds(aligned(block, LANES), LANES)] = rows[c : c + 1]

    pipelined(blocks, 2, gather, turn, True)


def exchange(rows, owners):
    blocks = rows.reshape(owners, 1, -1)
    blocks = lax.all_to_all(blocks, "gx", split_axis=0, concat_axis=0, tiled=True)
    return blocks.reshape(rows.shape)


def near_own(tiles):
    return pl.pallas_call(
        near_own_kernel,
        out_shape=jax.ShapeDtypeStruct(tiles.shape, F32),
        in_specs=[VMEM],
        out_specs=VMEM,
        compiler_params=params(),
        cost_estimate=pl.CostEstimate(flops=10**10, transcendentals=0, bytes_accessed=10**7),
        name="near1",
    )(tiles)


def near_others(places, previous, following, tiles, before):
    return pl.pallas_call(
        near_others_kernel,
        out_shape=jax.ShapeDtypeStruct(tiles.shape, F32),
        in_specs=[SMEM, ANY, ANY, VMEM, VMEM],
        out_specs=VMEM,
        scratch_shapes=[
            pltpu.VMEM((3 * tiles.shape[0], LANES), F32),
            pltpu.SemaphoreType.DMA((3,)),
        ],
        compiler_params=params(),
        cost_estimate=pl.CostEstimate(flops=2 * 10**10, transcendentals=0, bytes_accessed=10**7),
        name="near2",
    )(places, previous, following, tiles, before)


def halo(shard, devices):
    up = [(i, i + 1) for i in range(devices - 1)]
    down = [(i + 1, i) for i in range(devices - 1)]
    return lax.ppermute(shard, "gx", up), lax.ppermute(shard, "gx", down)


def body(
    positions,
    forces,
    deriv_mat,
    quad_mat,
    point_dest,
    leaf_center,
    tile_src,
    neighbours,
    inter_leaf,
    inter_op,
    coarse_op,
    up_pinv,
    trans_ops,
    child_ops,
):
    owners = lax.axis_size("gx")
    count = positions.shape[2]
    leaves = leaf_center.shape[2]
    slots = leaves * TILE
    expansion = up_pinv.shape[0]
    shape = jax.ShapeDtypeStruct
    first = lax.axis_index("gx") * leaves - leaves

    tangent = jnp.dot(
        positions.reshape(-1, P_SIZE), deriv_mat, precision=HIGHEST, preferred_element_type=F32
    ).reshape(3, count)
    jacobian = jnp.sqrt(1.0 + jnp.sum(tangent * tangent, axis=0))
    weighted = jnp.dot(
        forces.reshape(-1, P_SIZE), quad_mat, precision=HIGHEST, preferred_element_type=F32
    ).reshape(3, count)
    strengths = jnp.pad(weighted * jacobian[None], ((0, 2), (0, 0)))
    outgoing = pl.pallas_call(
        send_kernel,
        out_shape=shape((6 * slots // LANES, LANES), F32),
        in_specs=[SMEM, VMEM, VMEM],
        out_specs=VMEM,
        scratch_shapes=[pltpu.VMEM((slots, LANES), F32), pltpu.VMEM((4 * TILE, LANES), F32)],
        compiler_params=params(),
        name="send",
    )(point_dest.reshape(count), positions, strengths)
    arrived = exchange(outgoing, owners)

    source = tile_src.reshape(slots)
    centers = leaf_center.reshape(3 * leaves)
    sphere = RADIUS * sphere_points(SURF)
    surf_rows = jnp.pad(sphere, ((0, 5), (0, LANES - SURF)))
    surface = jnp.broadcast_to(surf_rows[:3, :SURF_PAD, None], (3, SURF_PAD, LANES))
    tiles, checks = pl.pallas_call(
        receive_kernel,
        out_shape=[shape((8 * leaves, LANES), F32), shape((3 * leaves, LANES), F32)],
        in_specs=[SMEM, SMEM, VMEM, VMEM, VMEM],
        out_specs=[VMEM, VMEM],
        scratch_shapes=[
            pltpu.VMEM((slots + 8, LANES), F32),
            pltpu.VMEM((2 * RECEIVE_GROUP * TILE, LANES), F32),
            pltpu.VMEM((2 * RECEIVE_GROUP * 32, LANES), F32),
        ],
        compiler_params=params(),
        name="receive",
    )(source, centers, arrived, surface, surf_rows)

    check = checks.reshape(leaves, 3, LANES)[:, :, :SURF].reshape(leaves, expansion)
    multipole = jnp.dot(check, up_pinv, precision=HIGHEST, preferred_element_type=F32)
    halves = [multipole[:, :LANES], jnp.pad(multipole[:, LANES:], ((0, 0), (0, 2 * LANES - expansion)))]
    grouped = jnp.sum(multipole.reshape(leaves // 8, 8, expansion), axis=0)
    moment = jnp.einsum("ce,cef->f", grouped, child_ops, precision=HIGHEST)
    moment = jnp.pad(moment, (0, 8 * LANES - expansion)).reshape(8, LANES)
    moment, *halves = lax.optimization_barrier((moment, *halves))
    coarse = lax.all_gather(moment, ("gx", "gy"), axis=0, tiled=True)
    previous, following = halo(jnp.concatenate([tiles] + halves, axis=0), owners)

    near = near_own(tiles)
    places = (neighbours[0, 1:] - first).reshape(2 * leaves)
    near = near_others(places, previous, following, tiles, near)
    sides = [previous[8 * leaves :], following[8 * leaves :]]
    multipole_ext = jnp.concatenate(
        [
            jnp.concatenate([sides[0][:leaves], halves[0], sides[1][:leaves]], axis=0),
            jnp.concatenate([sides[0][leaves:], halves[1], sides[1][leaves:]], axis=0),
        ],
        axis=1,
    )
    op_ids = jnp.arange(NOPS)
    picked = jnp.take(multipole_ext, (inter_leaf[0] - first).T, axis=0)[:, :, :expansion]
    leaf_hot = (inter_op[0].T[:, :, None] == op_ids[None, None, :]).astype(F32)
    leaf_by_op = jnp.einsum("nje,njk->nke", picked, leaf_hot, precision=HIGHEST)
    local = jnp.dot(
        leaf_by_op.reshape(leaves, NOPS * expansion),
        trans_ops.reshape(NOPS * expansion, expansion),
        precision=HIGHEST,
        preferred_element_type=F32,
    ).reshape(leaves, 3, SURF)
    local = jnp.pad(local, ((0, 0), (0, 0), (0, LANES - SURF))).reshape(3 * leaves, LANES)

    near, local, coarse = lax.optimization_barrier((near, local, coarse))
    coarse = coarse.reshape(-1, 8, LANES)[:, :2].reshape(-1, 2 * LANES)[:, :expansion]
    onehot = (coarse_op[0, 0][:, None] == op_ids[None, :]).astype(F32)
    by_op = jnp.einsum("bk,be->ke", onehot, coarse, precision=HIGHEST)
    coarse_local = jnp.einsum("ke,kef->f", by_op, trans_ops, precision=HIGHEST)
    pushed = jnp.einsum("cfe,e->cf", child_ops, coarse_local, precision=HIGHEST)
    pushed = jnp.pad(pushed.reshape(8, 3, SURF), ((0, 0), (0, 0), (0, LANES - SURF)))
    pushed = pushed.reshape(24, LANES)

    returning = pl.pallas_call(
        far_kernel,
        out_shape=shape((3 * slots // LANES, LANES), F32),
        in_specs=[SMEM, SMEM, VMEM, VMEM, VMEM, VMEM, VMEM, VMEM],
        out_specs=VMEM,
        scratch_shapes=[
            pltpu.VMEM((slots + 8, LANES), F32),
            pltpu.VMEM((2 * GROUP * TILE, LANES), F32),
            pltpu.VMEM((2 * GROUP * 40, LANES), F32),
        ],
        compiler_params=params(),
        name="far",
    )(source, centers, tiles, near, local, pushed, surface, surf_rows)
    came_back = exchange(returning, owners)
    velocity = pl.pallas_call(
        return_kernel,
        out_shape=shape((3, 1, count), F32),
        in_specs=[SMEM, VMEM],
        out_specs=VMEM,
        scratch_shapes=[pltpu.VMEM((slots, LANES), F32), pltpu.VMEM((4 * TILE, LANES), F32)],
        compiler_params=params(),
        name="back",
    )(point_dest.reshape(count), came_back)
    return velocity


def solution(mesh):
    in_specs = (
        P(None, "gy", "gx"),
        P(None, "gy", "gx"),
        P(),
        P(),
        P("gy", "gx"),
        P(None, "gy", "gx"),
        P("gy", "gx"),
        P("gy", None, "gx"),
        P("gy", None, "gx"),
        P("gy", None, "gx"),
        P("gy", "gx", None),
        P(),
        P(),
        P(),
    )
    out_specs = P(None, "gy", "gx")
    return jax.shard_map(body, mesh=mesh, in_specs=in_specs, out_specs=out_specs, check_vma=False)
```
